512 devices in a mesh: chan: 32 (over y, x), facet: 16 (over z, core).
Axes of the slice: x: 4, y: 8, z: 8, core: 2. Of those that a mesh axis runs over, the one named last changes fastest.
Arguments:
- start_image: float32 [64, 8192], P(None, 'facet'), may hold values from 0 to 3
- visibilities: bfloat16 [512, 64, 16, 256], P(('chan', 'facet')), may hold values from -12 to 12
- strip_index: int32 [512, 64, 16, 2], P(('chan', 'facet')), may hold values from 0 to 4095
- live_counts: int32 [512, 64, 16], P(('chan', 'facet')), may hold values from 0 to 128
- uv_kernels: bfloat16 [64, 16, 256, 256], P('chan', 'facet'), may hold values from -0.375 to 0.375
Outputs:
- final_image: float32 [64, 8192], P(None, 'facet')
The draws below stay inside these ranges and needn't reach their ends.
Inputs may be any that keep to these rules, and one draw needn't show every extreme that they name: `strip_index`: each visibility block reads 2 image strips. The first live_counts of a block's 128 visibilities are live, the others are flagged.
All inputs are finite; a program needn't handle non-finite values.
Results may differ from the reference program's by a relative error of at most 0.0026.
Values may be sent and summed in bfloat16 or wider, within the bound.
A program may use at most 64 MiB of HBM per device.

```python
import jax
import jax.numpy as jnp
from jax import lax

NPIX = 8192
STRIP = 128
VISB = 128
TERMS = 2
ITERS = 2
SLAB = 64
CHANNELS = 64
UVT = 16
SLOTS = 512
STRIPS = 4096


def with_ends(entries, stream_key, least, top_value):
    index_at = [jax.random.randint(jax.random.fold_in(stream_key, axis), (), 0, length) for axis, length in enumerate(entries.shape)]
    main_axis = entries.shape.index(max(entries.shape))
    beside = index_at[:main_axis] + [(index_at[main_axis] + 1) % entries.shape[main_axis]] + index_at[main_axis + 1:]
    return entries.at[tuple(index_at)].set(least).at[tuple(beside)].set(top_value)


def block_levels(rng, dims, cuts, low, top_value):
    def one(position, blocks):
        heights = jax.random.uniform(jax.random.fold_in(jax.random.fold_in(rng, 6), position), (blocks,), jnp.float32, low / len(cuts), top_value / len(cuts))
        return jnp.repeat(jnp.exp(heights), dims[position] // blocks).reshape((-1,) + (1,) * (len(dims) - position - 1))

    loudness = one(*cuts[0])
    for cut in cuts[1:]:
        loudness = loudness * one(*cut)
    return loudness


def noise(own_key, shape, scale, limit, cuts=(), held_as=jnp.bfloat16):
    level = block_levels(own_key, shape, cuts, -0.22, 0.18) if cuts else 1.0
    values = jax.random.normal(own_key, shape, jnp.float32) * scale * level
    return jnp.minimum(jnp.maximum(values, -limit), limit).astype(held_as)


def setup_inputs(seed: int = 0) -> dict:
    key_of = jax.random.split(jax.random.key(seed), 6)
    start_image = jnp.clip(3.0 * jax.random.uniform(key_of[0], (SLAB, NPIX), jnp.float32) ** block_levels(key_of[0], (SLAB, NPIX), ((1, 16),), -0.2, 0.2), 0.0, 3.0)
    visibilities = noise(key_of[1], (SLOTS, CHANNELS, UVT, 2 * VISB), 2.0, 12.0, ((0, 512),))
    strip_index = with_ends(jax.random.randint(key_of[2], (SLOTS, CHANNELS, UVT, TERMS), 0, STRIPS), jax.random.fold_in(key_of[2], 1), 0, STRIPS - 1).astype(jnp.int32)
    live_counts = with_ends(jax.random.randint(key_of[3], (SLOTS, CHANNELS, UVT), 0, VISB + 1), jax.random.fold_in(key_of[3], 1), 0, VISB).astype(jnp.int32)
    uv_kernels = noise(key_of[4], (CHANNELS, UVT, TERMS * STRIP, 2 * VISB), (TERMS * STRIP) ** -0.5, 0.375, ((0, 32), (1, 16)))
    return dict(start_image=start_image, visibilities=visibilities, strip_index=strip_index, live_counts=live_counts, uv_kernels=uv_kernels)


shrinkage = 0.05


def reference(start_image, visibilities, strip_index, live_counts, uv_kernels):
    strip_count = SLAB * NPIX // STRIP
    step_size = strip_count / (2.5 * SLOTS * CHANNELS * UVT)
    lane_ids = jnp.arange(2 * VISB, dtype=jnp.int32) % VISB
    estimate = start_image
    for iteration in range(ITERS):
        sky_strips = estimate.astype(jnp.bfloat16).reshape(strip_count, STRIP)

        def per_channel(channel, gradient):
            observed = lax.dynamic_index_in_dim(visibilities, channel, 1, keepdims=False)
            picked_ids = lax.dynamic_index_in_dim(strip_index, channel, 1, keepdims=False)
            live_now = lax.dynamic_index_in_dim(live_counts, channel, 1, keepdims=False)
            kernel_now = lax.dynamic_index_in_dim(uv_kernels, channel, 0, keepdims=False)
            gathered = sky_strips[picked_ids].reshape(SLOTS, UVT, TERMS * STRIP).astype(jnp.float32)
            kernel_wide = kernel_now.astype(jnp.float32)
            predicted = jnp.einsum("sup,upq->suq", gathered, kernel_wide)
            live_mask = lane_ids[None, None, :] < live_now[:, :, None]
            residual = jnp.where(live_mask, predicted - observed.astype(jnp.float32), jnp.float32(0.0)).astype(jnp.bfloat16)
            adjoint = jnp.einsum("suq,upq->sup", residual.astype(jnp.float32), kernel_wide)
            return gradient.at[picked_ids.reshape(-1)].add(adjoint.reshape(-1, STRIP))

        gradient = lax.fori_loop(0, CHANNELS, per_channel, jnp.zeros((strip_count, STRIP), jnp.float32))
        descent = estimate - step_size * gradient.reshape(SLAB, NPIX)
        estimate = jnp.maximum(descent - shrinkage, jnp.float32(0.0))
    return estimate
```

```python
import jax
import jax.numpy as jnp
from jax import lax
from jax.experimental import pallas as pl
from jax.experimental.pallas import tpu as pltpu
from jax.sharding import PartitionSpec as P

STRIP = 128
VISB = 128
TERMS = 2
ITERS = 2
NX = 4
NY = 8
NZ = 8
PLANE = NY * NZ
OWNERS = 2 * NX * PLANE
PIECE = 8

shrinkage = 0.05
MESH = pl.DeviceIdType.MESH


def reduce_kernel(
    final, step_size, g_ref, est_ref, out_ref, est_out, got1, sum1, got2, sum2, got3, sky, sems1, sems2, sems3, sems4, sems5, sems6
):
    chan = lax.axis_index("chan")
    facet = lax.axis_index("facet")
    y, x = chan // NX, chan % NX
    z, core = facet // 2, facet % 2
    spot = y * NZ + z

    partner = (chan, z * 2 + (1 - core))

    def on_x(dx):
        return (y * NX + lax.rem(x + dx, NX), facet)

    def on_plane(k):
        yy = lax.rem(y + k // NZ, NY)
        zz = lax.rem(z + k % NZ, NZ)
        return yy * NZ + zz, (yy * NX + x, zz * 2 + core)

    def on_chan(k):
        yy = lax.rem(y + k // NX, NY)
        xx = lax.rem(x + k % NX, NX)
        return (yy * NX + xx, facet)

    def copy(src, dst, send, recv, target):
        return pltpu.make_async_remote_copy(
            src_ref=src, dst_ref=dst, send_sem=send, recv_sem=recv, device_id=target, device_id_type=MESH
        )

    barrier = pltpu.get_barrier_semaphore()
    pl.semaphore_signal(barrier, inc=1, device_id=partner, device_id_type=MESH)
    for dx in range(1, NX):
        pl.semaphore_signal(barrier, inc=1, device_id=on_x(dx), device_id_type=MESH)

    @pl.loop(1, PLANE)
    def _(k):
        pl.semaphore_signal(barrier, inc=1, device_id=on_plane(k)[1], device_id_type=MESH)

    greeted = 1 + (NX - 1) + (PLANE - 1)
    if final:

        @pl.loop(1, NY)
        def _(dy):
            for dx in range(1, NX):
                pl.semaphore_signal(barrier, inc=1, device_id=on_chan(dy * NX + dx), device_id_type=MESH)

        greeted += (NY - 1) * (NX - 1)
    pl.semaphore_wait(barrier, greeted)

    order = [1, 3, 2, 0]

    def own_block(xx):
        return pl.ds((core * NX + xx) * PLANE, PLANE)

    def pair_copy(dx):
        xx = lax.rem(x + dx, NX)
        return copy(
            g_ref.at[pl.ds(((1 - core) * NX + xx) * PLANE, PLANE)],
            got1.at[dx],
            sems1.at[0, dx],
            sems1.at[1, dx],
            partner,
        )

    for dx in order:
        pair_copy(dx).start()

    def x_copy(dx):
        return copy(sum1.at[dx], got2.at[dx], sems2.at[0, dx], sems2.at[1, dx], on_x(dx))

    for dx in order[:-1]:
        pair_copy(dx).wait_recv()
        base = (core * NX + lax.rem(x + dx, NX)) * PLANE

        @pl.loop(0, PLANE // 8)
        def _(i):
            total = g_ref[pl.ds(base + i * 8, 8)].astype(jnp.float32) + got1[dx, pl.ds(i * 8, 8)].astype(jnp.float32)
            sum1[dx, pl.ds(i * 8, 8)] = total.astype(jnp.bfloat16)

        x_copy(dx).start()
    pair_copy(0).wait_recv()
    for dx in order[:-1]:
        x_copy(dx).wait_recv()
    base = (core * NX + x) * PLANE

    @pl.loop(0, PLANE // 8)
    def _(i):
        rows = pl.ds(i * 8, 8)
        total = g_ref[pl.ds(base + i * 8, 8)].astype(jnp.float32) + got1[0, rows].astype(jnp.float32)
        for dx in order[:-1]:
            total += got2[dx, rows].astype(jnp.float32)
        sum2[rows] = total.astype(jnp.bfloat16)

    def plane_copy(k):
        place, target = on_plane(k)
        return copy(sum2.at[place], got3.at[k], sems3.at[0, k], sems3.at[1, k], target)

    @pl.loop(1, PLANE)
    def _(k):
        plane_copy(k).start()

    @pl.loop(1, PLANE)
    def _(k):
        plane_copy(k).wait_recv()

    gradient = sum2[spot].astype(jnp.float32)
    for k in range(1, PLANE):
        gradient += got3[k].astype(jnp.float32)
    estimate = jnp.maximum(est_ref[...] - step_size * gradient - shrinkage, 0.0)

    if final:
        sky[chan] = estimate

        def chan_copy(k):
            return copy(sky.at[chan], sky.at[chan], sems4.at[0, k], sems4.at[1, k], on_chan(k))

        @pl.loop(1, NY * NX)
        def _(k):
            chan_copy(k).start()

        @pl.loop(1, NY * NX)
        def _(k):
            chan_copy(k).wait()

        out_ref[...] = sky[...]
        est_out[...] = estimate
    else:
        est_out[...] = estimate
        mine = (core * NX + x) * PLANE + spot
        sky[mine] = estimate.astype(jnp.bfloat16)

        def spread_plane(k):
            return copy(sky.at[mine], sky.at[mine], sems4.at[0, k], sems4.at[1, k], on_plane(k)[1])

        @pl.loop(1, PLANE)
        def _(k):
            spread_plane(k).start()

        @pl.loop(1, PLANE)
        def _(k):
            spread_plane(k).wait_recv()

        def spread_x(dx):
            block = sky.at[own_block(x)]
            return copy(block, block, sems5.at[0, dx], sems5.at[1, dx], on_x(dx))

        def spread_pair(dx):
            block = sky.at[own_block(lax.rem(x + dx, NX))]
            return copy(block, block, sems6.at[0, dx], sems6.at[1, dx], partner)

        for dx in order[:-1]:
            spread_x(dx).start()
        spread_pair(0).start()
        for dx in order[:-1]:
            spread_x(dx).wait_recv()
            spread_pair(NX - dx).start()
        for dx in range(NX):
            spread_pair(dx).wait()
        for dx in order[:-1]:
            spread_x(dx).wait_send()

        @pl.loop(1, PLANE)
        def _(k):
            spread_plane(k).wait_send()

        out_ref[...] = sky[...]

    for dx in order:
        pair_copy(dx).wait_send()
    for dx in order[:-1]:
        x_copy(dx).wait_send()

    @pl.loop(1, PLANE)
    def _(k):
        plane_copy(k).wait_send()


def reduce_step(final, step_size, gradient, estimate):
    def body(*refs):
        reduce_kernel(final, step_size, *refs)

    dma = pltpu.SemaphoreType.DMA
    if final:
        out = jax.ShapeDtypeStruct((NY * NX, PIECE, STRIP), jnp.float32)
    else:
        out = jax.ShapeDtypeStruct((OWNERS, PIECE, STRIP), jnp.bfloat16)
    return pl.pallas_call(
        body,
        out_shape=(out, jax.ShapeDtypeStruct((PIECE, STRIP), jnp.float32)),
        in_specs=[pl.BlockSpec(memory_space=pltpu.VMEM)] * 2,
        out_specs=(pl.BlockSpec(memory_space=pltpu.VMEM),) * 2,
        scratch_shapes=[
            pltpu.VMEM((NX, PLANE, PIECE, STRIP), jnp.bfloat16),
            pltpu.VMEM((NX, PLANE, PIECE, STRIP), jnp.bfloat16),
            pltpu.VMEM((NX, PLANE, PIECE, STRIP), jnp.bfloat16),
            pltpu.VMEM((PLANE, PIECE, STRIP), jnp.bfloat16),
            pltpu.VMEM((PLANE, PIECE, STRIP), jnp.bfloat16),
            pltpu.VMEM(out.shape, out.dtype),
            dma((2, NX)),
            dma((2, NX)),
            dma((2, PLANE)),
            dma((2, PLANE)),
            dma((2, NX)),
            dma((2, NX)),
        ],
        compiler_params=pltpu.CompilerParams(collective_id=1 if final else 0, has_side_effects=True),
        name="reduce_final" if final else "reduce_sky",
    )(gradient, estimate)


def owner_order(strip):
    quarter = strip % 4
    core = strip // 4 % 2
    z = strip // 8 % 8
    low_row = strip // 64 % 2
    x = strip // 128 % 4
    y = strip // 512
    return (((core * NX + x) * NY + y) * NZ + z) * PIECE + low_row * 4 + quarter


def on_device(start_image, visibilities, strip_index, live_counts, uv_kernels):
    observed, picked_ids, live_now = (
        lax.all_to_all(
            lax.all_to_all(array, "chan", split_axis=1, concat_axis=0, tiled=True),
            "facet",
            split_axis=2,
            concat_axis=0,
            tiled=True,
        )
        for array in (visibilities, owner_order(strip_index), live_counts)
    )
    chan_count = lax.axis_size("chan")
    facet_count = lax.axis_size("facet")
    slot_count = observed.shape[0]
    chan_local = uv_kernels.shape[0]
    uv_local = uv_kernels.shape[1]
    all_channels = chan_local * chan_count
    all_uvtiles = uv_local * facet_count
    slab_rows = start_image.shape[0]
    facet_width = start_image.shape[1]
    strip_count = slab_rows * facet_width * facet_count // STRIP
    step_size = strip_count / (2.5 * slot_count * all_channels * all_uvtiles)
    lane_ids = jnp.arange(2 * VISB, dtype=jnp.int32) % VISB
    live_mask = lane_ids < live_now[..., None]
    flat_ids = picked_ids.reshape(-1)
    pieces = start_image.reshape(NY * NX, PIECE, STRIP)
    estimate = lax.dynamic_index_in_dim(pieces, lax.axis_index("chan"), 0, keepdims=False)
    sky = lax.all_gather(start_image.astype(jnp.bfloat16), "facet", axis=0, tiled=False)
    sky = sky.reshape(NZ, 2, NY, NX, 2, 4, STRIP).transpose(1, 3, 2, 0, 4, 5, 6)
    for iteration in range(ITERS):
        sky_strips = sky.reshape(strip_count, STRIP)
        gathered = sky_strips[picked_ids].reshape(slot_count, chan_local, uv_local, TERMS * STRIP)
        predicted = jnp.einsum(
            "scup,cupq->scuq", gathered, uv_kernels, preferred_element_type=jnp.float32
        )
        residual = jnp.where(live_mask, predicted - observed.astype(jnp.float32), 0.0).astype(
            jnp.bfloat16
        )
        adjoint = jnp.einsum(
            "scuq,cupq->scup", residual, uv_kernels, preferred_element_type=jnp.float32
        )
        gradient = (
            jnp.zeros((strip_count, STRIP), jnp.float32)
            .at[flat_ids]
            .add(adjoint.reshape(-1, STRIP))
        )
        gradient = gradient.astype(jnp.bfloat16).reshape(OWNERS, PIECE, STRIP)
        sky, estimate = reduce_step(iteration == ITERS - 1, step_size, gradient, estimate)
    return sky.reshape(slab_rows, facet_width)


def solution(mesh):
    placed = (
        P(None, "facet"),
        P(("chan", "facet"), None, None, None),
        P(("chan", "facet"), None, None, None),
        P(("chan", "facet"), None, None),
        P("chan", "facet", None, None),
    )
    return jax.shard_map(
        on_device, mesh=mesh, in_specs=placed, out_specs=P(None, "facet"), check_vma=False
    )
```

```python
import jax
import jax.numpy as jnp
from jax import lax
from jax.experimental import pallas as pl
from jax.experimental.pallas import tpu as pltpu
from jax.sharding import PartitionSpec as P

STRIP = 128
VISB = 128
TERMS = 2
ITERS = 2
NX = 4
NY = 8
NZ = 8
PLANE = NY * NZ
OWNERS = 2 * NX * PLANE
PIECE = 8
NEAR = 2 * NX

FLAGGED = 1024.0

shrinkage = 0.05
MESH = pl.DeviceIdType.MESH


def exchange_kernel(
    start_ref,
    meta_ref,
    vis_ref,
    sky_out,
    index_out,
    vis_out,
    sky,
    meta1,
    packed,
    index_in,
    vis1,
    vis_in,
    sky_plane,
    sky_x,
    sky_pair,
    meta_near,
    meta_plane,
    vis_near,
    vis_plane,
):
    chan = lax.axis_index("chan")
    facet = lax.axis_index("facet")
    y, x = chan // NX, chan % NX
    z, core = facet // 2, facet % 2
    spot = y * NZ + z

    def near(i):
        cc = lax.rem(core + i // NX, 2)
        xx = lax.rem(x + i % NX, NX)
        return cc * NX + xx, (y * NX + xx, z * 2 + cc)

    def on_plane(k):
        yy = lax.rem(y + k // NZ, NY)
        zz = lax.rem(z + k % NZ, NZ)
        return yy * NZ + zz, (yy * NX + x, zz * 2 + core)

    def copy(src, dst, sems, at, target):
        return pltpu.make_async_remote_copy(
            src_ref=src,
            dst_ref=dst,
            send_sem=sems.at[0, at],
            recv_sem=sems.at[1, at],
            device_id=target,
            device_id_type=MESH,
        )

    barrier = pltpu.get_barrier_semaphore()
    for i in range(1, NEAR):
        pl.semaphore_signal(barrier, inc=1, device_id=near(i)[1], device_id_type=MESH)

    @pl.loop(1, PLANE)
    def _(k):
        pl.semaphore_signal(barrier, inc=1, device_id=on_plane(k)[1], device_id_type=MESH)

    pl.semaphore_wait(barrier, NEAR - 1 + PLANE - 1)

    def spread_plane(k):
        return copy(start_ref, sky.at[near(0)[0] * PLANE + spot], sky_plane, k, on_plane(k)[1])

    def own_block(xx):
        return sky.at[pl.ds((core * NX + xx) * PLANE, PLANE)]

    def spread_x(dx):
        return copy(own_block(x), own_block(x), sky_x, dx, near(dx)[1])

    def spread_pair(dx):
        block = own_block(lax.rem(x + dx, NX))
        return copy(block, block, sky_pair, dx, near(NX)[1])

    def near_meta(i):
        return copy(meta_ref.at[near(i)[0]], meta1.at[i], meta_near, i, near(i)[1])

    def near_vis(i):
        block = vis_ref.at[pl.ds(near(i)[0] * PLANE, PLANE)]
        return copy(block, vis1.at[pl.ds(i * PLANE, PLANE)], vis_near, i, near(i)[1])

    def plane_meta(k):
        place, target = on_plane(k)
        return copy(packed.at[place], index_in.at[k], meta_plane, k, target)

    @pl.loop(1, PLANE)
    def _(k):
        spread_plane(k).start()

    for i in range(1, NEAR):
        near_meta(i).start()
    for i in range(1, NEAR):
        near_vis(i).start()

    def forward(i):
        if i == 0:
            base = near(0)[0] * PLANE
            held = vis_ref
        else:
            base = i * PLANE
            held = vis1
        vis_in[0, i] = held[base + spot]

        @pl.loop(1, PLANE)
        def _(k):
            place, target = on_plane(k)
            copy(held.at[base + place], vis_in.at[k, i], vis_plane, 0, target).start()

    for i in range(1, NEAR):
        near_meta(i).wait_recv()
    lane = lax.broadcasted_iota(jnp.int32, (32, STRIP), 1)
    place = lax.broadcasted_iota(jnp.int32, (32, STRIP), 0)
    belongs = lane // 4 == place
    column = lax.broadcasted_iota(jnp.int32, (STRIP, STRIP), 1)
    source = lax.broadcasted_iota(jnp.int32, (STRIP, STRIP), 0)
    total = jnp.zeros((4 * 32, STRIP), jnp.float32)
    for i in range(NEAR):
        strips = meta_ref[near(0)[0]] if i == 0 else meta1[i]
        high = jnp.floor(strips * (1.0 / 64.0))
        low = strips - 64.0 * high
        spread = jnp.concatenate(
            [
                jnp.where(belongs, jnp.broadcast_to(part[h : h + 1], (32, STRIP)), 0.0)
                for part in (high, low)
                for h in range(2)
            ],
            axis=0,
        )
        move = jnp.where(column == 4 * i + source % 4, 1.0, 0.0).astype(jnp.bfloat16)
        total += jnp.dot(spread.astype(jnp.bfloat16), move, preferred_element_type=jnp.float32)
    rows = 64.0 * total[:64] + total[64:]
    for d in range(PLANE):
        packed[d] = rows[d : d + 1]
    index_in[0] = packed[spot]

    @pl.loop(1, PLANE)
    def _(k):
        plane_meta(k).start()

    sky[near(0)[0] * PLANE + spot] = start_ref[...]

    @pl.loop(1, PLANE)
    def _(k):
        spread_plane(k).wait_recv()

    for dx in range(1, NX):
        spread_x(dx).start()
    spread_pair(0).start()
    forward(0)
    for i in range(1, NEAR):
        if i < NX:
            spread_x(i).wait_recv()
            spread_pair(NX - i).start()
        near_vis(i).wait_recv()
        forward(i)

    @pl.loop(1, PLANE)
    def _(k):
        plane_meta(k).wait()

    for dx in range(NX):
        spread_pair(dx).wait()
    sky_out[...] = sky[...]
    index_out[...] = index_in[...]
    arrived = vis_in.at[pl.ds(1, PLANE - 1)]
    copy(arrived, arrived, vis_plane, 0, near(NX)[1]).wait()
    vis_out[...] = vis_in[...]
    for dx in range(1, NX):
        spread_x(dx).wait_send()
    for i in range(1, NEAR):
        near_meta(i).wait_send()
        near_vis(i).wait_send()

    @pl.loop(1, PLANE)
    def _(k):
        spread_plane(k).wait_send()


def exchange(start_piece, strips, visibilities):
    dma = pltpu.SemaphoreType.DMA
    vmem = pltpu.VMEM
    sky = (OWNERS, PIECE, STRIP)
    index = (PLANE, 1, STRIP)
    blocks = (PLANE, NEAR, 4, STRIP)
    return pl.pallas_call(
        exchange_kernel,
        out_shape=(
            jax.ShapeDtypeStruct(sky, jnp.bfloat16),
            jax.ShapeDtypeStruct(index, jnp.float32),
            jax.ShapeDtypeStruct(blocks, jnp.bfloat16),
        ),
        in_specs=[pl.BlockSpec(memory_space=vmem)] * 3,
        out_specs=(pl.BlockSpec(memory_space=vmem),) * 3,
        scratch_shapes=[
            vmem(sky, jnp.bfloat16),
            vmem((NEAR, 2, STRIP), jnp.float32),
            vmem(index, jnp.float32),
            vmem(index, jnp.float32),
            vmem((NEAR * PLANE, 4, STRIP), jnp.bfloat16),
            vmem(blocks, jnp.bfloat16),
            dma((2, PLANE)),
            dma((2, NX)),
            dma((2, NX)),
            dma((2, NEAR)),
            dma((2, PLANE)),
            dma((2, NEAR)),
            dma((2, 1)),
        ],
        compiler_params=pltpu.CompilerParams(collective_id=2, has_side_effects=True),
        name="exchange",
    )(start_piece, strips, visibilities)


def reduce_kernel(
    final, step_size, g_ref, est_ref, out_ref, est_out, got1, sum1, got2, sum2, got3, sky, sems1, sems2, sems3, sems4, sems5, sems6
):
    chan = lax.axis_index("chan")
    facet = lax.axis_index("facet")
    y, x = chan // NX, chan % NX
    z, core = facet // 2, facet % 2
    spot = y * NZ + z

    partner = (chan, z * 2 + (1 - core))

    def on_x(dx):
        return (y * NX + lax.rem(x + dx, NX), facet)

    def on_plane(k):
        yy = lax.rem(y + k // NZ, NY)
        zz = lax.rem(z + k % NZ, NZ)
        return yy * NZ + zz, (yy * NX + x, zz * 2 + core)

    def on_chan(k):
        yy = lax.rem(y + k // NX, NY)
        xx = lax.rem(x + k % NX, NX)
        return (yy * NX + xx, facet)

    def copy(src, dst, send, recv, target):
        return pltpu.make_async_remote_copy(
            src_ref=src, dst_ref=dst, send_sem=send, recv_sem=recv, device_id=target, device_id_type=MESH
        )

    barrier = pltpu.get_barrier_semaphore()
    pl.semaphore_signal(barrier, inc=1, device_id=partner, device_id_type=MESH)
    for dx in range(1, NX):
        pl.semaphore_signal(barrier, inc=1, device_id=on_x(dx), device_id_type=MESH)

    @pl.loop(1, PLANE)
    def _(k):
        pl.semaphore_signal(barrier, inc=1, device_id=on_plane(k)[1], device_id_type=MESH)

    greeted = 1 + (NX - 1) + (PLANE - 1)
    if final:

        @pl.loop(1, NY)
        def _(dy):
            for dx in range(1, NX):
                pl.semaphore_signal(barrier, inc=1, device_id=on_chan(dy * NX + dx), device_id_type=MESH)

        greeted += (NY - 1) * (NX - 1)
    pl.semaphore_wait(barrier, greeted)

    order = [1, 3, 2, 0]

    def own_block(xx):
        return pl.ds((core * NX + xx) * PLANE, PLANE)

    def pair_copy(dx):
        xx = lax.rem(x + dx, NX)
        return copy(
            g_ref.at[pl.ds(((1 - core) * NX + xx) * PLANE, PLANE)],
            got1.at[dx],
            sems1.at[0, dx],
            sems1.at[1, dx],
            partner,
        )

    for dx in order:
        pair_copy(dx).start()

    def x_copy(dx):
        return copy(sum1.at[dx], got2.at[dx], sems2.at[0, dx], sems2.at[1, dx], on_x(dx))

    for dx in order[:-1]:
        pair_copy(dx).wait_recv()
        base = (core * NX + lax.rem(x + dx, NX)) * PLANE

        @pl.loop(0, PLANE // 8)
        def _(i):
            total = g_ref[pl.ds(base + i * 8, 8)].astype(jnp.float32) + got1[dx, pl.ds(i * 8, 8)].astype(jnp.float32)
            sum1[dx, pl.ds(i * 8, 8)] = total.astype(jnp.bfloat16)

        x_copy(dx).start()
    pair_copy(0).wait_recv()
    for dx in order[:-1]:
        x_copy(dx).wait_recv()
    base = (core * NX + x) * PLANE

    @pl.loop(0, PLANE // 8)
    def _(i):
        rows = pl.ds(i * 8, 8)
        total = g_ref[pl.ds(base + i * 8, 8)].astype(jnp.float32) + got1[0, rows].astype(jnp.float32)
        for dx in order[:-1]:
            total += got2[dx, rows].astype(jnp.float32)
        sum2[rows] = total.astype(jnp.bfloat16)

    def plane_copy(k):
        place, target = on_plane(k)
        return copy(sum2.at[place], got3.at[k], sems3.at[0, k], sems3.at[1, k], target)

    @pl.loop(1, PLANE)
    def _(k):
        plane_copy(k).start()

    @pl.loop(1, PLANE)
    def _(k):
        plane_copy(k).wait_recv()

    gradient = sum2[spot].astype(jnp.float32)
    for k in range(1, PLANE):
        gradient += got3[k].astype(jnp.float32)
    estimate = jnp.maximum(est_ref[...] - step_size * gradient - shrinkage, 0.0)

    if final:
        sky[chan] = estimate

        def chan_copy(k):
            return copy(sky.at[chan], sky.at[chan], sems4.at[0, k], sems4.at[1, k], on_chan(k))

        @pl.loop(1, NY * NX)
        def _(k):
            chan_copy(k).start()

        @pl.loop(1, NY * NX)
        def _(k):
            chan_copy(k).wait()

        out_ref[...] = sky[...]
        est_out[...] = estimate
    else:
        est_out[...] = estimate
        mine = (core * NX + x) * PLANE + spot
        sky[mine] = estimate.astype(jnp.bfloat16)

        def spread_plane(k):
            return copy(sky.at[mine], sky.at[mine], sems4.at[0, k], sems4.at[1, k], on_plane(k)[1])

        @pl.loop(1, PLANE)
        def _(k):
            spread_plane(k).start()

        @pl.loop(1, PLANE)
        def _(k):
            spread_plane(k).wait_recv()

        def spread_x(dx):
            block = sky.at[own_block(x)]
            return copy(block, block, sems5.at[0, dx], sems5.at[1, dx], on_x(dx))

        def spread_pair(dx):
            block = sky.at[own_block(lax.rem(x + dx, NX))]
            return copy(block, block, sems6.at[0, dx], sems6.at[1, dx], partner)

        for dx in order[:-1]:
            spread_x(dx).start()
        spread_pair(0).start()
        for dx in order[:-1]:
            spread_x(dx).wait_recv()
            spread_pair(NX - dx).start()
        for dx in range(NX):
            spread_pair(dx).wait()
        for dx in order[:-1]:
            spread_x(dx).wait_send()

        @pl.loop(1, PLANE)
        def _(k):
            spread_plane(k).wait_send()

        out_ref[...] = sky[...]

    for dx in order:
        pair_copy(dx).wait_send()
    for dx in order[:-1]:
        x_copy(dx).wait_send()

    @pl.loop(1, PLANE)
    def _(k):
        plane_copy(k).wait_send()


def reduce_step(final, step_size, gradient, estimate):
    def body(*refs):
        reduce_kernel(final, step_size, *refs)

    dma = pltpu.SemaphoreType.DMA
    if final:
        out = jax.ShapeDtypeStruct((NY * NX, PIECE, STRIP), jnp.float32)
    else:
        out = jax.ShapeDtypeStruct((OWNERS, PIECE, STRIP), jnp.bfloat16)
    return pl.pallas_call(
        body,
        out_shape=(out, jax.ShapeDtypeStruct((PIECE, STRIP), jnp.float32)),
        in_specs=[pl.BlockSpec(memory_space=pltpu.VMEM)] * 2,
        out_specs=(pl.BlockSpec(memory_space=pltpu.VMEM),) * 2,
        scratch_shapes=[
            pltpu.VMEM((NX, PLANE, PIECE, STRIP), jnp.bfloat16),
            pltpu.VMEM((NX, PLANE, PIECE, STRIP), jnp.bfloat16),
            pltpu.VMEM((NX, PLANE, PIECE, STRIP), jnp.bfloat16),
            pltpu.VMEM((PLANE, PIECE, STRIP), jnp.bfloat16),
            pltpu.VMEM((PLANE, PIECE, STRIP), jnp.bfloat16),
            pltpu.VMEM(out.shape, out.dtype),
            dma((2, NX)),
            dma((2, NX)),
            dma((2, PLANE)),
            dma((2, PLANE)),
            dma((2, NX)),
            dma((2, NX)),
        ],
        compiler_params=pltpu.CompilerParams(collective_id=1 if final else 0, has_side_effects=True),
        name="reduce_final" if final else "reduce_sky",
    )(gradient, estimate)


def owner_order(strip):
    quarter = strip % 4
    core = strip // 4 % 2
    z = strip // 8 % 8
    low_row = strip // 64 % 2
    x = strip // 128 % 4
    y = strip // 512
    return (((core * NX + x) * NY + y) * NZ + z) * PIECE + low_row * 4 + quarter


def on_device(start_image, visibilities, strip_index, live_counts, uv_kernels):
    slot_count = lax.axis_size("chan") * lax.axis_size("facet")
    channels, uvtiles = visibilities.shape[1:3]
    slab_rows, facet_width = start_image.shape
    strip_count = OWNERS * PIECE
    chan_local, uv_local = uv_kernels.shape[:2]
    step_size = strip_count / (2.5 * slot_count * channels * uvtiles)

    lane_ids = jnp.arange(2 * VISB, dtype=jnp.int32) % VISB
    live_mask = lane_ids < live_counts[..., None]
    marked = jnp.where(live_mask, visibilities, jnp.bfloat16(FLAGGED))
    marked = marked.reshape(NY, NX, 2, NZ, 2, 2, STRIP).transpose(4, 1, 0, 3, 2, 5, 6)
    strips = owner_order(strip_index).astype(jnp.float32)
    strips = strips.reshape(NY, NX, 2, NZ, 2, 2).transpose(4, 1, 0, 3, 2, 5)
    pieces = start_image.reshape(NY * NX, PIECE, STRIP)
    estimate = lax.dynamic_index_in_dim(pieces, lax.axis_index("chan"), 0, keepdims=False)
    sky, picked, observed = exchange(
        estimate.astype(jnp.bfloat16),
        strips.reshape(NEAR, 2, STRIP),
        marked.reshape(OWNERS, 4, STRIP),
    )
    picked_ids = picked[:, 0, : 4 * NEAR].astype(jnp.int32).reshape(slot_count, chan_local, uv_local, TERMS)
    flat_ids = picked_ids.reshape(-1)
    observed = observed.reshape(slot_count, chan_local, uv_local, 2 * VISB)
    for iteration in range(ITERS):
        sky_strips = sky.reshape(strip_count, STRIP)
        gathered = sky_strips[picked_ids].reshape(slot_count, chan_local, uv_local, TERMS * STRIP)
        predicted = jnp.einsum(
            "scup,cupq->scuq", gathered, uv_kernels, preferred_element_type=jnp.float32
        )
        residual = jnp.where(observed < FLAGGED, predicted - observed.astype(jnp.float32), 0.0).astype(
            jnp.bfloat16
        )
        adjoint = jnp.einsum(
            "scuq,cupq->scup", residual, uv_kernels, preferred_element_type=jnp.float32
        )
        gradient = (
            jnp.zeros((strip_count, STRIP), jnp.float32)
            .at[flat_ids]
            .add(adjoint.reshape(-1, STRIP))
        )
        gradient = gradient.astype(jnp.bfloat16).reshape(OWNERS, PIECE, STRIP)
        sky, estimate = reduce_step(iteration == ITERS - 1, step_size, gradient, estimate)
    return sky.reshape(slab_rows, facet_width)


def solution(mesh):
    placed = (
        P(None, "facet"),
        P(("chan", "facet"), None, None, None),
        P(("chan", "facet"), None, None, None),
        P(("chan", "facet"), None, None),
        P("chan", "facet", None, None),
    )
    return jax.shard_map(
        on_device, mesh=mesh, in_specs=placed, out_specs=P(None, "facet"), check_vma=False
    )
```

```python
import jax
import jax.numpy as jnp
from jax import lax
from jax.experimental import pallas as pl
from jax.experimental.pallas import tpu as pltpu
from jax.sharding import PartitionSpec as P

STRIP = 128
VISB = 128
TERMS = 2
ITERS = 2
NX = 4
NY = 8
NZ = 8
PLANE = NY * NZ
OWNERS = 2 * NX * PLANE
PIECE = 8
NEAR = 2 * NX

FLAGGED = 1024.0

shrinkage = 0.05
MESH = pl.DeviceIdType.MESH


def exchange_kernel(
    start_ref,
    meta_ref,
    vis_ref,
    sky_out,
    index_out,
    vis_out,
    sky,
    meta1,
    packed,
    index_in,
    vis1,
    vis_in,
    sky_plane,
    sky_x,
    sky_pair,
    meta_near,
    meta_plane,
    vis_near,
    vis_plane,
):
    chan = lax.axis_index("chan")
    facet = lax.axis_index("facet")
    y, x = chan // NX, chan % NX
    z, core = facet // 2, facet % 2
    spot = y * NZ + z

    def near(i):
        cc = lax.rem(core + i // NX, 2)
        xx = lax.rem(x + i % NX, NX)
        return cc * NX + xx, (y * NX + xx, z * 2 + cc)

    def on_plane(k):
        yy = lax.rem(y + k // NZ, NY)
        zz = lax.rem(z + k % NZ, NZ)
        return yy * NZ + zz, (yy * NX + x, zz * 2 + core)

    def copy(src, dst, sems, at, target):
        return pltpu.make_async_remote_copy(
            src_ref=src,
            dst_ref=dst,
            send_sem=sems.at[0, at],
            recv_sem=sems.at[1, at],
            device_id=target,
            device_id_type=MESH,
        )

    barrier = pltpu.get_barrier_semaphore()
    for i in range(1, NEAR):
        pl.semaphore_signal(barrier, inc=1, device_id=near(i)[1], device_id_type=MESH)

    @pl.loop(1, PLANE)
    def _(k):
        pl.semaphore_signal(barrier, inc=1, device_id=on_plane(k)[1], device_id_type=MESH)

    pl.semaphore_wait(barrier, NEAR - 1 + PLANE - 1)

    def spread_plane(k):
        return copy(start_ref, sky.at[near(0)[0] * PLANE + spot], sky_plane, k, on_plane(k)[1])

    def own_block(xx):
        return sky.at[pl.ds((core * NX + xx) * PLANE, PLANE)]

    def spread_x(dx):
        return copy(own_block(x), own_block(x), sky_x, dx, near(dx)[1])

    def spread_pair(dx):
        block = own_block(lax.rem(x + dx, NX))
        return copy(block, block, sky_pair, dx, near(NX)[1])

    def near_meta(i):
        return copy(meta_ref.at[near(i)[0]], meta1.at[i], meta_near, i, near(i)[1])

    def near_vis(i):
        block = vis_ref.at[pl.ds(near(i)[0] * PLANE, PLANE)]
        return copy(block, vis1.at[pl.ds(i * PLANE, PLANE)], vis_near, i, near(i)[1])

    def plane_meta(k):
        place, target = on_plane(k)
        return copy(packed.at[place], index_in.at[k], meta_plane, k, target)

    @pl.loop(1, PLANE)
    def _(k):
        spread_plane(k).start()

    for i in range(1, NEAR):
        near_meta(i).start()
    for i in range(1, NEAR):
        near_vis(i).start()

    def forward(i):
        if i == 0:
            base = near(0)[0] * PLANE
            held = vis_ref
        else:
            base = i * PLANE
            held = vis1
        vis_in[0, i] = held[base + spot]

        @pl.loop(1, PLANE)
        def _(k):
            place, target = on_plane(k)
            copy(held.at[base + place], vis_in.at[k, i], vis_plane, 0, target).start()

    for i in range(1, NEAR):
        near_meta(i).wait_recv()
    lane = lax.broadcasted_iota(jnp.int32, (32, STRIP), 1)
    place = lax.broadcasted_iota(jnp.int32, (32, STRIP), 0)
    belongs = lane // 4 == place
    column = lax.broadcasted_iota(jnp.int32, (STRIP, STRIP), 1)
    source = lax.broadcasted_iota(jnp.int32, (STRIP, STRIP), 0)
    total = jnp.zeros((4 * 32, STRIP), jnp.float32)
    for i in range(NEAR):
        strips = meta_ref[near(0)[0]] if i == 0 else meta1[i]
        high = jnp.floor(strips * (1.0 / 64.0))
        low = strips - 64.0 * high
        spread = jnp.concatenate(
            [
                jnp.where(belongs, jnp.broadcast_to(part[h : h + 1], (32, STRIP)), 0.0)
                for part in (high, low)
                for h in range(2)
            ],
            axis=0,
        )
        move = jnp.where(column == 4 * i + source % 4, 1.0, 0.0).astype(jnp.bfloat16)
        total += jnp.dot(spread.astype(jnp.bfloat16), move, preferred_element_type=jnp.float32)
    rows = 64.0 * total[:64] + total[64:]
    for d in range(PLANE):
        packed[d] = rows[d : d + 1]
    index_in[0] = packed[spot]

    @pl.loop(1, PLANE)
    def _(k):
        plane_meta(k).start()

    sky[near(0)[0] * PLANE + spot] = start_ref[...]

    @pl.loop(1, PLANE)
    def _(k):
        spread_plane(k).wait_recv()

    for dx in range(1, NX):
        spread_x(dx).start()
    spread_pair(0).start()
    forward(0)
    for i in range(1, NEAR):
        if i < NX:
            spread_x(i).wait_recv()
            spread_pair(NX - i).start()
        near_vis(i).wait_recv()
        forward(i)

    @pl.loop(1, PLANE)
    def _(k):
        plane_meta(k).wait()

    for dx in range(NX):
        spread_pair(dx).wait()
    sky_out[...] = sky[...]
    index_out[...] = index_in[...].astype(jnp.int32)
    arrived = vis_in.at[pl.ds(1, PLANE - 1)]
    copy(arrived, arrived, vis_plane, 0, near(NX)[1]).wait()
    vis_out[...] = vis_in[...]
    for dx in range(1, NX):
        spread_x(dx).wait_send()
    for i in range(1, NEAR):
        near_meta(i).wait_send()
        near_vis(i).wait_send()

    @pl.loop(1, PLANE)
    def _(k):
        spread_plane(k).wait_send()


def exchange(start_piece, strips, visibilities):
    dma = pltpu.SemaphoreType.DMA
    vmem = pltpu.VMEM
    sky = (OWNERS, PIECE, STRIP)
    index = (PLANE, 1, STRIP)
    blocks = (PLANE, NEAR, 4, STRIP)
    return pl.pallas_call(
        exchange_kernel,
        out_shape=(
            jax.ShapeDtypeStruct(sky, jnp.bfloat16),
            jax.ShapeDtypeStruct(index, jnp.int32),
            jax.ShapeDtypeStruct(blocks, jnp.bfloat16),
        ),
        in_specs=[pl.BlockSpec(memory_space=vmem)] * 3,
        out_specs=(pl.BlockSpec(memory_space=vmem),) * 3,
        scratch_shapes=[
            vmem(sky, jnp.bfloat16),
            vmem((NEAR, 2, STRIP), jnp.float32),
            vmem(index, jnp.float32),
            vmem(index, jnp.float32),
            vmem((NEAR * PLANE, 4, STRIP), jnp.bfloat16),
            vmem(blocks, jnp.bfloat16),
            dma((2, PLANE)),
            dma((2, NX)),
            dma((2, NX)),
            dma((2, NEAR)),
            dma((2, PLANE)),
            dma((2, NEAR)),
            dma((2, 1)),
        ],
        compiler_params=pltpu.CompilerParams(collective_id=2, has_side_effects=True),
        name="exchange",
    )(start_piece, strips, visibilities)


def reduce_kernel(
    final, step_size, g_ref, est_ref, out_ref, est_out, got1, sum1, got2, sum2, got3, sky, sems1, sems2, sems3, sems4, sems5, sems6
):
    chan = lax.axis_index("chan")
    facet = lax.axis_index("facet")
    y, x = chan // NX, chan % NX
    z, core = facet // 2, facet % 2
    spot = y * NZ + z

    partner = (chan, z * 2 + (1 - core))

    def on_x(dx):
        return (y * NX + lax.rem(x + dx, NX), facet)

    def on_plane(k):
        yy = lax.rem(y + k // NZ, NY)
        zz = lax.rem(z + k % NZ, NZ)
        return yy * NZ + zz, (yy * NX + x, zz * 2 + core)

    def on_chan(k):
        yy = lax.rem(y + k // NX, NY)
        xx = lax.rem(x + k % NX, NX)
        return (yy * NX + xx, facet)

    def copy(src, dst, send, recv, target):
        return pltpu.make_async_remote_copy(
            src_ref=src, dst_ref=dst, send_sem=send, recv_sem=recv, device_id=target, device_id_type=MESH
        )

    barrier = pltpu.get_barrier_semaphore()
    pl.semaphore_signal(barrier, inc=1, device_id=partner, device_id_type=MESH)
    for dx in range(1, NX):
        pl.semaphore_signal(barrier, inc=1, device_id=on_x(dx), device_id_type=MESH)

    @pl.loop(1, PLANE)
    def _(k):
        pl.semaphore_signal(barrier, inc=1, device_id=on_plane(k)[1], device_id_type=MESH)

    greeted = 1 + (NX - 1) + (PLANE - 1)
    if final:

        @pl.loop(1, NY)
        def _(dy):
            for dx in range(1, NX):
                pl.semaphore_signal(barrier, inc=1, device_id=on_chan(dy * NX + dx), device_id_type=MESH)

        greeted += (NY - 1) * (NX - 1)
    pl.semaphore_wait(barrier, greeted)

    order = [1, 3, 2, 0]

    def own_block(xx):
        return pl.ds((core * NX + xx) * PLANE, PLANE)

    def pair_copy(dx):
        xx = lax.rem(x + dx, NX)
        return copy(
            g_ref.at[pl.ds(((1 - core) * NX + xx) * PLANE, PLANE)],
            got1.at[dx],
            sems1.at[0, dx],
            sems1.at[1, dx],
            partner,
        )

    for dx in order:
        pair_copy(dx).start()

    def x_copy(dx):
        return copy(sum1.at[dx], got2.at[dx], sems2.at[0, dx], sems2.at[1, dx], on_x(dx))

    for dx in order[:-1]:
        pair_copy(dx).wait_recv()
        base = (core * NX + lax.rem(x + dx, NX)) * PLANE

        @pl.loop(0, PLANE // 8)
        def _(i):
            total = g_ref[pl.ds(base + i * 8, 8)].astype(jnp.float32) + got1[dx, pl.ds(i * 8, 8)].astype(jnp.float32)
            sum1[dx, pl.ds(i * 8, 8)] = total.astype(jnp.bfloat16)

        x_copy(dx).start()
    pair_copy(0).wait_recv()
    for dx in order[:-1]:
        x_copy(dx).wait_recv()
    base = (core * NX + x) * PLANE

    @pl.loop(0, PLANE // 8)
    def _(i):
        rows = pl.ds(i * 8, 8)
        total = g_ref[pl.ds(base + i * 8, 8)].astype(jnp.float32) + got1[0, rows].astype(jnp.float32)
        for dx in order[:-1]:
            total += got2[dx, rows].astype(jnp.float32)
        sum2[rows] = total.astype(jnp.bfloat16)

    def plane_copy(k):
        place, target = on_plane(k)
        return copy(sum2.at[place], got3.at[k], sems3.at[0, k], sems3.at[1, k], target)

    @pl.loop(1, PLANE)
    def _(k):
        plane_copy(k).start()

    @pl.loop(1, PLANE)
    def _(k):
        plane_copy(k).wait_recv()

    gradient = sum2[spot].astype(jnp.float32)
    for k in range(1, PLANE):
        gradient += got3[k].astype(jnp.float32)
    estimate = jnp.maximum(est_ref[...] - step_size * gradient - shrinkage, 0.0)

    if final:
        sky[chan] = estimate

        def chan_copy(k):
            return copy(sky.at[chan], sky.at[chan], sems4.at[0, k], sems4.at[1, k], on_chan(k))

        @pl.loop(1, NY * NX)
        def _(k):
            chan_copy(k).start()

        @pl.loop(1, NY * NX)
        def _(k):
            chan_copy(k).wait()

        out_ref[...] = sky[...]
        est_out[...] = estimate
    else:
        est_out[...] = estimate
        mine = (core * NX + x) * PLANE + spot
        sky[mine] = estimate.astype(jnp.bfloat16)

        def spread_plane(k):
            return copy(sky.at[mine], sky.at[mine], sems4.at[0, k], sems4.at[1, k], on_plane(k)[1])

        @pl.loop(1, PLANE)
        def _(k):
            spread_plane(k).start()

        @pl.loop(1, PLANE)
        def _(k):
            spread_plane(k).wait_recv()

        def spread_x(dx):
            block = sky.at[own_block(x)]
            return copy(block, block, sems5.at[0, dx], sems5.at[1, dx], on_x(dx))

        def spread_pair(dx):
            block = sky.at[own_block(lax.rem(x + dx, NX))]
            return copy(block, block, sems6.at[0, dx], sems6.at[1, dx], partner)

        for dx in order[:-1]:
            spread_x(dx).start()
        spread_pair(0).start()
        for dx in order[:-1]:
            spread_x(dx).wait_recv()
            spread_pair(NX - dx).start()
        for dx in range(NX):
            spread_pair(dx).wait()
        for dx in order[:-1]:
            spread_x(dx).wait_send()

        @pl.loop(1, PLANE)
        def _(k):
            spread_plane(k).wait_send()

        out_ref[...] = sky[...]

    for dx in order:
        pair_copy(dx).wait_send()
    for dx in order[:-1]:
        x_copy(dx).wait_send()

    @pl.loop(1, PLANE)
    def _(k):
        plane_copy(k).wait_send()


def reduce_step(final, step_size, gradient, estimate):
    def body(*refs):
        reduce_kernel(final, step_size, *refs)

    dma = pltpu.SemaphoreType.DMA
    if final:
        out = jax.ShapeDtypeStruct((NY * NX, PIECE, STRIP), jnp.float32)
    else:
        out = jax.ShapeDtypeStruct((OWNERS, PIECE, STRIP), jnp.bfloat16)
    return pl.pallas_call(
        body,
        out_shape=(out, jax.ShapeDtypeStruct((PIECE, STRIP), jnp.float32)),
        in_specs=[pl.BlockSpec(memory_space=pltpu.VMEM)] * 2,
        out_specs=(pl.BlockSpec(memory_space=pltpu.VMEM),) * 2,
        scratch_shapes=[
            pltpu.VMEM((NX, PLANE, PIECE, STRIP), jnp.bfloat16),
            pltpu.VMEM((NX, PLANE, PIECE, STRIP), jnp.bfloat16),
            pltpu.VMEM((NX, PLANE, PIECE, STRIP), jnp.bfloat16),
            pltpu.VMEM((PLANE, PIECE, STRIP), jnp.bfloat16),
            pltpu.VMEM((PLANE, PIECE, STRIP), jnp.bfloat16),
            pltpu.VMEM(out.shape, out.dtype),
            dma((2, NX)),
            dma((2, NX)),
            dma((2, PLANE)),
            dma((2, PLANE)),
            dma((2, NX)),
            dma((2, NX)),
        ],
        compiler_params=pltpu.CompilerParams(collective_id=1 if final else 0, has_side_effects=True),
        name="reduce_final" if final else "reduce_sky",
    )(gradient, estimate)


def gradient_kernel(index_ref, sky_ref, vis_ref, kernel_ref, out_ref, strips, picked, adjoint, *sums):
    @pl.loop(0, OWNERS // 8)
    def _(i):
        block = sky_ref[pl.ds(i * 8, 8)].astype(jnp.float32)
        strips[pl.ds(pl.multiple_of(i * 64, 64), 64)] = block.reshape(64, STRIP)
        for total in sums:
            total[pl.ds(pl.multiple_of(i * 64, 64), 64)] = jnp.zeros((64, STRIP), jnp.float32)

    @pl.loop(0, PLANE)
    def _(k):
        for i in range(NEAR):
            for q in range(4):
                strip = index_ref[k, 0, 4 * i + q]
                picked[q, k, pl.ds(i, 1)] = strips[pl.ds(strip, 1)]

    for ch in range(2):
        weights = kernel_ref[ch, 0]
        gathered = jnp.concatenate(
            [picked[2 * ch + j].reshape(PLANE * NEAR, STRIP).astype(jnp.bfloat16) for j in range(TERMS)], axis=1
        )
        predicted = jnp.dot(gathered, weights, preferred_element_type=jnp.float32)
        observed = vis_ref[ch].astype(jnp.float32)
        residual = jnp.where(observed < FLAGGED, predicted - observed, 0.0).astype(jnp.bfloat16)
        back = lax.dot_general(residual, weights, (((1,), (1,)), ((), ())), preferred_element_type=jnp.float32)
        for j in range(TERMS):
            adjoint[2 * ch + j] = back[:, j * STRIP : (j + 1) * STRIP].reshape(PLANE, NEAR, STRIP)

    @pl.loop(0, PLANE)
    def _(k):
        for i in range(NEAR):
            for q in range(4):
                total = sums[(4 * i + q) % len(sums)]
                strip = index_ref[k, 0, 4 * i + q]
                total[pl.ds(strip, 1)] += adjoint[q, k, pl.ds(i, 1)]

    @pl.loop(0, OWNERS // 8)
    def _(i):
        rows = pl.ds(pl.multiple_of(i * 64, 64), 64)
        block = sums[0][rows]
        for total in sums[1:]:
            block += total[rows]
        out_ref[pl.ds(i * 8, 8)] = block.reshape(8, 8, STRIP).astype(jnp.bfloat16)


SUMS = 8


def gradient_step(index, sky, visibilities, kernels):
    vmem = pltpu.VMEM
    image = (OWNERS * PIECE, STRIP)
    rows = (4, PLANE, NEAR, STRIP)
    return pl.pallas_call(
        gradient_kernel,
        out_shape=jax.ShapeDtypeStruct((OWNERS, PIECE, STRIP), jnp.bfloat16),
        in_specs=[pl.BlockSpec(memory_space=pltpu.SMEM)] + [pl.BlockSpec(memory_space=vmem)] * 3,
        out_specs=pl.BlockSpec(memory_space=vmem),
        scratch_shapes=[vmem(image, jnp.float32), vmem(rows, jnp.float32), vmem(rows, jnp.float32)]
        + [vmem(image, jnp.float32)] * SUMS,
        name="gradient",
    )(index, sky, visibilities, kernels)


def owner_order(strip):
    quarter = strip % 4
    core = strip // 4 % 2
    z = strip // 8 % 8
    low_row = strip // 64 % 2
    x = strip // 128 % 4
    y = strip // 512
    return (((core * NX + x) * NY + y) * NZ + z) * PIECE + low_row * 4 + quarter


def on_device(start_image, visibilities, strip_index, live_counts, uv_kernels):
    slot_count = lax.axis_size("chan") * lax.axis_size("facet")
    channels, uvtiles = visibilities.shape[1:3]
    slab_rows, facet_width = start_image.shape
    strip_count = OWNERS * PIECE
    step_size = strip_count / (2.5 * slot_count * channels * uvtiles)

    lane_ids = jnp.arange(2 * VISB, dtype=jnp.int32) % VISB
    live_mask = lane_ids < live_counts[..., None]
    marked = jnp.where(live_mask, visibilities, jnp.bfloat16(FLAGGED))
    marked = marked.reshape(NY, NX, 2, NZ, 2, 2, STRIP).transpose(4, 1, 0, 3, 2, 5, 6)
    strips = owner_order(strip_index).astype(jnp.float32)
    strips = strips.reshape(NY, NX, 2, NZ, 2, 2).transpose(4, 1, 0, 3, 2, 5)
    pieces = start_image.reshape(NY * NX, PIECE, STRIP)
    estimate = lax.dynamic_index_in_dim(pieces, lax.axis_index("chan"), 0, keepdims=False)
    sky, picked, observed = exchange(
        estimate.astype(jnp.bfloat16),
        strips.reshape(NEAR, 2, STRIP),
        marked.reshape(OWNERS, 4, STRIP),
    )
    observed = observed.reshape(slot_count, 2, 2 * VISB).swapaxes(0, 1)
    for iteration in range(ITERS):
        gradient = gradient_step(picked, sky, observed, uv_kernels)
        sky, estimate = reduce_step(iteration == ITERS - 1, step_size, gradient, estimate)
    return sky.reshape(slab_rows, facet_width)


def solution(mesh):
    placed = (
        P(None, "facet"),
        P(("chan", "facet"), None, None, None),
        P(("chan", "facet"), None, None, None),
        P(("chan", "facet"), None, None),
        P("chan", "facet", None, None),
    )
    return jax.shard_map(
        on_device, mesh=mesh, in_specs=placed, out_specs=P(None, "facet"), check_vma=False
    )
```

```python
import jax
import jax.numpy as jnp
from jax import lax
from jax.experimental import pallas as pl
from jax.experimental.pallas import tpu as pltpu
from jax.sharding import PartitionSpec as P

STRIP = 128
VISB = 128
TERMS = 2
ITERS = 2
NX = 4
NY = 8
NZ = 8
PLANE = NY * NZ
OWNERS = 2 * NX * PLANE
PIECE = 8
NEAR = 2 * NX

FLAGGED = 1024.0

shrinkage = 0.05
MESH = pl.DeviceIdType.MESH


class Place:
    def __init__(self):
        chan = lax.axis_index("chan")
        facet = lax.axis_index("facet")
        self.chan, self.facet = chan, facet
        self.y, self.x = chan // NX, chan % NX
        self.z, self.core = facet // 2, facet % 2
        self.spot = self.y * NZ + self.z
        self.owner = self.core * NX + self.x
        self.ys = [lax.rem(self.y + d, NY) for d in range(NY)]
        self.zs = [lax.rem(self.z + d, NZ) for d in range(NZ)]
        self.xs = [lax.rem(self.x + d, NX) for d in range(NX)]
        self.chan_y = [yy * NX + self.x for yy in self.ys]
        self.facet_z = [zz * 2 + self.core for zz in self.zs]
        self.partner = (chan, self.z * 2 + (1 - self.core))

    def on_x(self, dx):
        return (self.y * NX + self.xs[dx], self.facet)

    def on_plane(self, dy, dz):
        return self.ys[dy] * NZ + self.zs[dz], (self.chan_y[dy], self.facet_z[dz])

    def on_chan(self, dy, dx):
        return (self.ys[dy] * NX + self.xs[dx], self.facet)

    def near(self, i):
        core = lax.rem(self.core + lax.rem(i, 2), 2)
        step = i // 2
        xx = lax.rem(self.x + step * (step + 1) // 2, NX)
        return core * NX + xx, (self.y * NX + xx, self.z * 2 + core)


def reach(d, length):
    return min(d, length - d)


FAR_FIRST = sorted(
    ((dy, dz) for dy in range(NY) for dz in range(NZ) if dy or dz),
    key=lambda step: -reach(step[0], NY) - reach(step[1], NZ),
)
CHAN_FAR_FIRST = sorted(
    ((dy, dx) for dy in range(NY) for dx in range(NX) if dy or dx),
    key=lambda step: -reach(step[0], NY) - reach(step[1], NX),
)


def remote(src, dst, sems, at, target):
    return pltpu.make_async_remote_copy(
        src_ref=src,
        dst_ref=dst,
        send_sem=sems.at[0, at],
        recv_sem=sems.at[1, at],
        device_id=target,
        device_id_type=MESH,
    )


def greet(targets):
    barrier = pltpu.get_barrier_semaphore()
    for target in targets:
        pl.semaphore_signal(barrier, inc=1, device_id=target, device_id_type=MESH)
    pl.semaphore_wait(barrier, len(targets))


def exchange_kernel(
    start_ref,
    meta_ref,
    vis_ref,
    sky_out,
    index_out,
    vis_out,
    sky,
    meta1,
    packed,
    index_in,
    vis1,
    vis_in,
    sky_plane,
    sky_x,
    sky_pair,
    meta_near,
    meta_plane,
    vis_near,
    vis_plane,
    own_sem,
):
    me = Place()
    own_sky = sky.at[me.owner * PLANE + me.spot]
    sky_copy = pltpu.make_async_copy(start_ref, own_sky, own_sem.at[0])
    sky_copy.start()
    vis_copy = pltpu.make_async_copy(
        vis_ref.at[pl.ds(me.owner * PLANE, PLANE)], vis1.at[pl.ds(0, PLANE)], own_sem.at[1]
    )
    vis_copy.start()
    greet([me.on_plane(dy, dz)[1] for dy, dz in FAR_FIRST] + [me.near(i)[1] for i in range(1, NEAR)])

    for dy, dz in FAR_FIRST:
        remote(start_ref, own_sky, sky_plane, 0, me.on_plane(dy, dz)[1]).start()

    def near_meta(i):
        return remote(meta_ref, meta1.at[i], meta_near, i, me.near(i)[1])

    def near_vis(i):
        owner, target = me.near(i)
        block = vis_ref.at[pl.ds(owner * PLANE, PLANE)]
        return remote(block, vis1.at[pl.ds(i * PLANE, PLANE)], vis_near, i, target)

    def own_block(xx):
        return sky.at[pl.ds((me.core * NX + xx) * PLANE, PLANE)]

    def spread_x(dx):
        return remote(own_block(me.x), own_block(me.x), sky_x, dx, me.on_x(dx))

    def spread_pair(dx):
        block = own_block(me.xs[dx])
        return remote(block, block, sky_pair, dx, me.partner)

    for i in range(1, NEAR):
        near_meta(i).start()
    for i in range(1, NEAR):
        near_vis(i).start()

    sky_copy.wait()
    vis_copy.wait()

    def forward(i):
        base = i * PLANE
        vis_in[0, i] = vis1[base + me.spot]
        for dy, dz in FAR_FIRST:
            place, target = me.on_plane(dy, dz)
            remote(vis1.at[base + place], vis_in.at[dy * NZ + dz, i], vis_plane, 0, target).start()

    forward(0)

    for i in range(1, NEAR):
        near_meta(i).wait_recv()
    lane = lax.broadcasted_iota(jnp.int32, (PLANE, STRIP), 1)
    place = lax.broadcasted_iota(jnp.int32, (PLANE, STRIP), 0)
    belongs = (lane // 2) == (place // NZ) * NX + me.x
    column = lax.broadcasted_iota(jnp.int32, (STRIP, STRIP), 1)
    source = lax.broadcasted_iota(jnp.int32, (STRIP, STRIP), 0)
    total = jnp.zeros((2 * PLANE, STRIP), jnp.float32)
    for i in range(NEAR):
        held = meta_ref if i == 0 else meta1.at[i]
        for j in range(TERMS):
            strips = held[pl.ds(me.core * 2 + j, NZ, stride=4)]
            high = strips // 64
            low = strips - 64 * high
            spread = jnp.concatenate(
                [
                    jnp.where(belongs, jnp.concatenate([part.astype(jnp.float32)] * NY, axis=0), 0.0)
                    for part in (high, low)
                ],
                axis=0,
            )
            move = jnp.where(column == 4 * i + 2 * (source % 2) + j, 1.0, 0.0).astype(jnp.bfloat16)
            total += jnp.dot(spread.astype(jnp.bfloat16), move, preferred_element_type=jnp.float32)
    rows = 64.0 * total[:PLANE] + total[PLANE:]
    for d in range(PLANE):
        packed[d] = rows[d : d + 1]
    index_in[0] = packed[me.spot]
    for dy, dz in FAR_FIRST:
        spot, target = me.on_plane(dy, dz)
        remote(packed.at[spot], index_in.at[dy * NZ + dz], meta_plane, 0, target).start()

    near_vis(1).wait_recv()
    forward(1)

    others = sky.at[pl.ds(0, PLANE - 1)]
    remote(others, others, sky_plane, 0, me.partner).wait_recv()
    for dx in (2, 1, 3):
        spread_x(dx).start()
    spread_pair(0).start()

    @pl.loop(2, NEAR)
    def _(i):
        near_vis(i).wait_recv()
        forward(i)

    for dx in (1, 3, 2):
        spread_x(dx).wait_recv()
        spread_pair(NX - dx).start()
    far_index = index_in.at[pl.ds(1, PLANE - 1)]
    remote(far_index, far_index, meta_plane, 0, me.partner).wait()
    index_out[...] = index_in[...].astype(jnp.int32)
    for dx in range(NX):
        spread_pair(dx).wait()
    sky_out[...] = sky[...]
    for dx in (1, 3, 2):
        spread_x(dx).wait_send()
    for i in range(1, NEAR):
        near_meta(i).wait_send()
        near_vis(i).wait_send()
    remote(others, others, sky_plane, 0, me.partner).wait_send()
    arrived = vis_in.at[pl.ds(1, PLANE - 1)]
    remote(arrived, arrived, vis_plane, 0, me.partner).wait()
    vis_out[...] = vis_in[...]


def exchange(start_piece, strips, visibilities):
    dma = pltpu.SemaphoreType.DMA
    vmem = pltpu.VMEM
    sky = (OWNERS, PIECE, STRIP)
    index = (PLANE, 1, STRIP)
    blocks = (PLANE, NEAR, 4, STRIP)
    return pl.pallas_call(
        exchange_kernel,
        out_shape=(
            jax.ShapeDtypeStruct(sky, jnp.bfloat16),
            jax.ShapeDtypeStruct(index, jnp.int32),
            jax.ShapeDtypeStruct(blocks, jnp.bfloat16),
        ),
        in_specs=[pl.BlockSpec(memory_space=vmem)] * 3,
        out_specs=(pl.BlockSpec(memory_space=vmem),) * 3,
        scratch_shapes=[
            vmem(sky, jnp.bfloat16),
            vmem((NEAR, NZ * 4, STRIP), jnp.int32),
            vmem(index, jnp.float32),
            vmem(index, jnp.float32),
            vmem((NEAR * PLANE, 4, STRIP), jnp.bfloat16),
            vmem(blocks, jnp.bfloat16),
            dma((2, 1)),
            dma((2, NX)),
            dma((2, NX)),
            dma((2, NEAR)),
            dma((2, 1)),
            dma((2, NEAR)),
            dma((2, 1)),
            dma((2,)),
        ],
        compiler_params=pltpu.CompilerParams(collective_id=2, has_side_effects=True),
        name="exchange",
    )(start_piece, strips, visibilities)


def reduce_kernel(
    final, step_size, g_ref, est_ref, out_ref, est_out, got1, sum1, got2, sum2, got3, sky, sems1, sems2, sems3, sems4, sems5, sems6
):
    me = Place()
    targets = [me.on_plane(dy, dz)[1] for dy, dz in FAR_FIRST]
    if final:
        targets += [me.on_chan(dy, dx) for dy, dx in CHAN_FAR_FIRST if dy and dx]
    greet(targets + [me.on_x(dx) for dx in (2, 1, 3)] + [me.partner])

    order = [1, 3, 2, 0]

    def own_block(xx):
        return pl.ds((me.core * NX + xx) * PLANE, PLANE)

    def pair_copy(dx):
        block = g_ref.at[pl.ds(((1 - me.core) * NX + me.xs[dx]) * PLANE, PLANE)]
        return remote(block, got1.at[dx], sems1, dx, me.partner)

    for dx in order:
        pair_copy(dx).start()

    def x_copy(dx):
        return remote(sum1.at[dx], got2.at[dx], sems2, dx, me.on_x(dx))

    for dx in order[:-1]:
        pair_copy(dx).wait_recv()
        base = (me.core * NX + me.xs[dx]) * PLANE

        @pl.loop(0, PLANE // 8)
        def _(i):
            total = g_ref[pl.ds(base + i * 8, 8)].astype(jnp.float32) + got1[dx, pl.ds(i * 8, 8)].astype(jnp.float32)
            sum1[dx, pl.ds(i * 8, 8)] = total.astype(jnp.bfloat16)

        x_copy(dx).start()
    pair_copy(0).wait_recv()
    for dx in order[:-1]:
        x_copy(dx).wait_recv()
    base = me.owner * PLANE

    @pl.loop(0, PLANE // 8)
    def _(i):
        rows = pl.ds(i * 8, 8)
        total = g_ref[pl.ds(base + i * 8, 8)].astype(jnp.float32) + got1[0, rows].astype(jnp.float32)
        for dx in order[:-1]:
            total += got2[dx, rows].astype(jnp.float32)
        sum2[rows] = total.astype(jnp.bfloat16)

    for dy, dz in FAR_FIRST:
        place, target = me.on_plane(dy, dz)
        remote(sum2.at[place], got3.at[dy * NZ + dz], sems3, 0, target).start()
    others = got3.at[pl.ds(1, PLANE - 1)]
    all_plane = remote(others, others, sems3, 0, me.partner)
    all_plane.wait_recv()

    parts = [sum2[me.spot].astype(jnp.float32)] + [jnp.zeros((PIECE, STRIP), jnp.float32) for _ in range(3)]
    for k in range(1, PLANE):
        parts[k % 4] += got3[k].astype(jnp.float32)
    gradient = (parts[0] + parts[1]) + (parts[2] + parts[3])
    estimate = jnp.maximum(est_ref[...] - step_size * gradient - shrinkage, 0.0)

    if final:
        mine = sky.at[pl.ds(pl.multiple_of(me.chan * PIECE, PIECE), PIECE)]
        mine[...] = estimate
        for dy, dx in CHAN_FAR_FIRST:
            remote(mine, mine, sems4, 0, me.on_chan(dy, dx)).start()
        est_out[...] = estimate
        rest = sky.at[pl.ds(0, (NY * NX - 1) * PIECE)]
        remote(rest, rest, sems4, 0, me.partner).wait()
        for quarter in range(4):
            out_ref[:, quarter * STRIP : (quarter + 1) * STRIP] = sky[pl.ds(quarter, 2 * NY * NX, stride=4)]
    else:
        mine = sky.at[me.owner * PLANE + me.spot]
        mine[...] = estimate.astype(jnp.bfloat16)
        for dy, dz in FAR_FIRST:
            remote(mine, mine, sems4, 0, me.on_plane(dy, dz)[1]).start()
        est_out[...] = estimate
        rest = sky.at[pl.ds(0, PLANE - 1)]
        all_sky = remote(rest, rest, sems4, 0, me.partner)
        all_sky.wait_recv()

        def spread_x(dx):
            block = sky.at[own_block(me.x)]
            return remote(block, block, sems5, dx, me.on_x(dx))

        def spread_pair(dx):
            block = sky.at[own_block(me.xs[dx])]
            return remote(block, block, sems6, dx, me.partner)

        for dx in (2, 1, 3):
            spread_x(dx).start()
        spread_pair(0).start()
        for dx in order[:-1]:
            spread_x(dx).wait_recv()
            spread_pair(NX - dx).start()
        for dx in range(NX):
            spread_pair(dx).wait()
        out_ref[...] = sky[...]
        for dx in order[:-1]:
            spread_x(dx).wait_send()
        all_sky.wait_send()

    for dx in order:
        pair_copy(dx).wait_send()
    for dx in order[:-1]:
        x_copy(dx).wait_send()
    all_plane.wait_send()


def reduce_step(final, step_size, gradient, estimate):
    def body(*refs):
        reduce_kernel(final, step_size, *refs)

    dma = pltpu.SemaphoreType.DMA
    if final:
        out = jax.ShapeDtypeStruct((2 * NY * NX, 4 * STRIP), jnp.float32)
        sky = pltpu.VMEM((NY * NX * PIECE, STRIP), jnp.float32)
    else:
        sky = pltpu.VMEM((OWNERS, PIECE, STRIP), jnp.bfloat16)
        out = jax.ShapeDtypeStruct((OWNERS, PIECE, STRIP), jnp.bfloat16)
    return pl.pallas_call(
        body,
        out_shape=(out, jax.ShapeDtypeStruct((PIECE, STRIP), jnp.float32)),
        in_specs=[pl.BlockSpec(memory_space=pltpu.VMEM)] * 2,
        out_specs=(pl.BlockSpec(memory_space=pltpu.VMEM),) * 2,
        scratch_shapes=[
            pltpu.VMEM((NX, PLANE, PIECE, STRIP), jnp.bfloat16),
            pltpu.VMEM((NX, PLANE, PIECE, STRIP), jnp.bfloat16),
            pltpu.VMEM((NX, PLANE, PIECE, STRIP), jnp.bfloat16),
            pltpu.VMEM((PLANE, PIECE, STRIP), jnp.bfloat16),
            pltpu.VMEM((PLANE, PIECE, STRIP), jnp.bfloat16),
            sky,
            dma((2, NX)),
            dma((2, NX)),
            dma((2, 1)),
            dma((2, 1)),
            dma((2, NX)),
            dma((2, NX)),
        ],
        compiler_params=pltpu.CompilerParams(collective_id=1 if final else 0, has_side_effects=True),
        name="reduce_final" if final else "reduce_sky",
    )(gradient, estimate)


def gradient_kernel(index_ref, sky_ref, vis_ref, kernel_ref, out_ref, strips, picked, adjoint, *sums):
    @pl.loop(0, OWNERS // 8)
    def _(i):
        block = sky_ref[pl.ds(i * 8, 8)].astype(jnp.float32)
        strips[pl.ds(pl.multiple_of(i * 64, 64), 64)] = block.reshape(64, STRIP)
        for total in sums:
            total[pl.ds(pl.multiple_of(i * 64, 64), 64)] = jnp.zeros((64, STRIP), jnp.float32)

    @pl.loop(0, PLANE)
    def _(k):
        for i in range(NEAR):
            for q in range(4):
                strip = index_ref[k, 0, 4 * i + q]
                picked[q, k, pl.ds(i, 1)] = strips[pl.ds(strip, 1)]

    for ch in range(2):
        weights = kernel_ref[ch, 0]
        gathered = jnp.concatenate(
            [picked[2 * ch + j].reshape(PLANE * NEAR, STRIP).astype(jnp.bfloat16) for j in range(TERMS)], axis=1
        )
        predicted = jnp.dot(gathered, weights, preferred_element_type=jnp.float32)
        observed = vis_ref[ch].astype(jnp.float32)
        residual = jnp.where(observed < FLAGGED, predicted - observed, 0.0).astype(jnp.bfloat16)
        back = lax.dot_general(residual, weights, (((1,), (1,)), ((), ())), preferred_element_type=jnp.float32)
        for j in range(TERMS):
            adjoint[2 * ch + j] = back[:, j * STRIP : (j + 1) * STRIP].reshape(PLANE, NEAR, STRIP)

    @pl.loop(0, PLANE)
    def _(k):
        for i in range(NEAR):
            for q in range(4):
                total = sums[(4 * i + q) % len(sums)]
                strip = index_ref[k, 0, 4 * i + q]
                total[pl.ds(strip, 1)] += adjoint[q, k, pl.ds(i, 1)]

    @pl.loop(0, OWNERS // 8)
    def _(i):
        rows = pl.ds(pl.multiple_of(i * 64, 64), 64)
        block = sums[0][rows]
        for total in sums[1:]:
            block += total[rows]
        out_ref[pl.ds(i * 8, 8)] = block.reshape(8, 8, STRIP).astype(jnp.bfloat16)


SUMS = 8


def gradient_step(index, sky, visibilities, kernels):
    vmem = pltpu.VMEM
    image = (OWNERS * PIECE, STRIP)
    rows = (4, PLANE, NEAR, STRIP)
    return pl.pallas_call(
        gradient_kernel,
        out_shape=jax.ShapeDtypeStruct((OWNERS, PIECE, STRIP), jnp.bfloat16),
        in_specs=[pl.BlockSpec(memory_space=pltpu.SMEM)] + [pl.BlockSpec(memory_space=vmem)] * 3,
        out_specs=pl.BlockSpec(memory_space=vmem),
        scratch_shapes=[vmem(image, jnp.float32), vmem(rows, jnp.float32), vmem(rows, jnp.float32)]
        + [vmem(image, jnp.float32)] * SUMS,
        name="gradient",
    )(index, sky, visibilities, kernels)


def owner_order(strip):
    quarter = strip % 4
    core = strip // 4 % 2
    z = strip // 8 % 8
    low_row = strip // 64 % 2
    x = strip // 128 % 4
    y = strip // 512
    return (((core * NX + x) * NY + y) * NZ + z) * PIECE + low_row * 4 + quarter


def on_device(start_image, visibilities, strip_index, live_counts, uv_kernels):
    slot_count = lax.axis_size("chan") * lax.axis_size("facet")
    channels, uvtiles = visibilities.shape[1:3]
    slab_rows, facet_width = start_image.shape
    strip_count = OWNERS * PIECE
    step_size = strip_count / (2.5 * slot_count * channels * uvtiles)

    lane_ids = jnp.arange(2 * VISB, dtype=jnp.int32) % VISB
    live_mask = lane_ids < live_counts[..., None]
    marked = jnp.where(live_mask, visibilities, jnp.bfloat16(FLAGGED))
    marked = marked.reshape(NY, NX, 2, NZ, 2, 2, STRIP).transpose(4, 1, 0, 3, 2, 5, 6)
    strips = owner_order(strip_index).transpose(0, 2, 3, 1).reshape(NZ * 4, channels)
    strips = jnp.pad(strips, ((0, 0), (0, STRIP - channels)))
    rows = lax.dynamic_slice_in_dim(start_image, lax.axis_index("chan") * 2, 2, 0)
    estimate = rows.reshape(PIECE, STRIP)
    sky, picked, observed = exchange(
        estimate.astype(jnp.bfloat16),
        strips,
        marked.reshape(OWNERS, 4, STRIP),
    )
    observed = observed.reshape(slot_count, 2, 2 * VISB).swapaxes(0, 1)
    for iteration in range(ITERS):
        gradient = gradient_step(picked, sky, observed, uv_kernels)
        sky, estimate = reduce_step(iteration == ITERS - 1, step_size, gradient, estimate)
    return sky


def solution(mesh):
    placed = (
        P(None, "facet"),
        P(("chan", "facet"), None, None, None),
        P(("chan", "facet"), None, None, None),
        P(("chan", "facet"), None, None),
        P("chan", "facet", None, None),
    )
    return jax.shard_map(
        on_device, mesh=mesh, in_specs=placed, out_specs=P(None, "facet"), check_vma=False
    )
```

```python
import jax
import jax.numpy as jnp
from jax import lax
from jax.experimental import pallas as pl
from jax.experimental.pallas import tpu as pltpu
from jax.sharding import PartitionSpec as P

STRIP = 128
VISB = 128
TERMS = 2
ITERS = 2
NX = 4
NY = 8
NZ = 8
PLANE = NY * NZ
OWNERS = 2 * NX * PLANE
PIECE = 8
NEAR = 2 * NX
GROUP = 4 * NEAR
BLOCKS = PLANE * NEAR
READS = 4 * BLOCKS
HALF = 64

FLAGGED = 1024.0

shrinkage = 0.05
MESH = pl.DeviceIdType.MESH


class Place:
    def __init__(self):
        chan = lax.axis_index("chan")
        facet = lax.axis_index("facet")
        self.chan, self.facet = chan, facet
        self.y, self.x = chan // NX, chan % NX
        self.z, self.core = facet // 2, facet % 2
        self.spot = self.y * NZ + self.z
        self.owner = self.core * NX + self.x
        self.ys = [lax.rem(self.y + d, NY) for d in range(NY)]
        self.zs = [lax.rem(self.z + d, NZ) for d in range(NZ)]
        self.xs = [lax.rem(self.x + d, NX) for d in range(NX)]
        self.chan_y = [yy * NX + self.x for yy in self.ys]
        self.facet_z = [zz * 2 + self.core for zz in self.zs]
        self.partner = (chan, self.z * 2 + (1 - self.core))

    def on_x(self, dx):
        return (self.y * NX + self.xs[dx], self.facet)

    def on_plane(self, dy, dz):
        return self.ys[dy] * NZ + self.zs[dz], (self.chan_y[dy], self.facet_z[dz])

    def on_chan(self, dy, dx):
        return (self.ys[dy] * NX + self.xs[dx], self.facet)

    def near(self, i):
        core = lax.rem(self.core + lax.rem(i, 2), 2)
        step = i // 2
        xx = lax.rem(self.x + step * (step + 1) // 2, NX)
        return core * NX + xx, (self.y * NX + xx, self.z * 2 + core)


def reach(d, length):
    return min(d, length - d)


FAR_FIRST = sorted(
    ((dy, dz) for dy in range(NY) for dz in range(NZ) if dy or dz),
    key=lambda step: -reach(step[0], NY) - reach(step[1], NZ),
)
CHAN_FAR_FIRST = sorted(
    ((dy, dx) for dy in range(NY) for dx in range(NX) if dy or dx),
    key=lambda step: -reach(step[0], NY) - reach(step[1], NX),
)


def remote(src, dst, sems, at, target):
    return pltpu.make_async_remote_copy(
        src_ref=src,
        dst_ref=dst,
        send_sem=sems.at[0, at],
        recv_sem=sems.at[1, at],
        device_id=target,
        device_id_type=MESH,
    )


def greet(targets):
    barrier = pltpu.get_barrier_semaphore()
    for target in targets:
        pl.semaphore_signal(barrier, inc=1, device_id=target, device_id_type=MESH)
    return lambda: pl.semaphore_wait(barrier, len(targets))


def exchange_kernel(
    start_ref,
    meta_ref,
    vis_ref,
    sky_out,
    index_out,
    vis_out,
    sky,
    meta1,
    packed,
    index_in,
    vis1,
    vis_in,
    sky_plane,
    sky_x,
    sky_pair,
    meta_near,
    meta_plane,
    vis_near,
    vis_plane,
    own_sem,
):
    me = Place()
    own_sky = sky.at[me.owner * PLANE + me.spot]
    sky_copy = pltpu.make_async_copy(start_ref, own_sky, own_sem.at[0])
    sky_copy.start()
    vis_copy = pltpu.make_async_copy(
        vis_ref.at[pl.ds(me.owner * PLANE, PLANE)], vis1.at[pl.ds(0, PLANE)], own_sem.at[1]
    )
    vis_copy.start()
    greet([me.on_plane(dy, dz)[1] for dy, dz in FAR_FIRST] + [me.near(i)[1] for i in range(1, NEAR)])()

    for dy, dz in FAR_FIRST:
        remote(start_ref, own_sky, sky_plane, 0, me.on_plane(dy, dz)[1]).start()

    def near_meta(i):
        return remote(meta_ref, meta1.at[i], meta_near, i, me.near(i)[1])

    def near_vis(i):
        owner, target = me.near(i)
        block = vis_ref.at[pl.ds(owner * PLANE, PLANE)]
        return remote(block, vis1.at[pl.ds(i * PLANE, PLANE)], vis_near, i, target)

    def own_block(xx):
        return sky.at[pl.ds((me.core * NX + xx) * PLANE, PLANE)]

    def spread_x(dx):
        return remote(own_block(me.x), own_block(me.x), sky_x, dx, me.on_x(dx))

    def spread_pair(dx):
        block = own_block(me.xs[dx])
        return remote(block, block, sky_pair, dx, me.partner)

    for i in range(1, NEAR):
        near_meta(i).start()
    for i in range(1, NEAR):
        near_vis(i).start()

    sky_copy.wait()
    vis_copy.wait()

    def forward(i):
        base = i * PLANE
        vis_in[0, i] = vis1[base + me.spot]
        for dy, dz in FAR_FIRST:
            place, target = me.on_plane(dy, dz)
            remote(vis1.at[base + place], vis_in.at[dy * NZ + dz, i], vis_plane, 0, target).start()

    forward(0)

    for i in range(1, NEAR):
        near_meta(i).wait_recv()
    lane = lax.broadcasted_iota(jnp.int32, (PLANE, STRIP), 1)
    place = lax.broadcasted_iota(jnp.int32, (PLANE, STRIP), 0)
    belongs = (lane // 2) == (place // NZ) * NX + me.x
    column = lax.broadcasted_iota(jnp.int32, (STRIP, STRIP), 1)
    source = lax.broadcasted_iota(jnp.int32, (STRIP, STRIP), 0)
    total = jnp.zeros((2 * PLANE, STRIP), jnp.float32)
    for i in range(NEAR):
        held = meta_ref if i == 0 else meta1.at[i]
        for j in range(TERMS):
            strips = held[pl.ds(me.core * 2 + j, NZ, stride=4)]
            high = strips // 64
            low = strips - 64 * high
            spread = jnp.concatenate(
                [
                    jnp.where(belongs, jnp.concatenate([part.astype(jnp.float32)] * NY, axis=0), 0.0)
                    for part in (high, low)
                ],
                axis=0,
            )
            move = jnp.where(column % GROUP == 4 * i + 2 * (source % 2) + j, 1.0, 0.0).astype(jnp.bfloat16)
            total += jnp.dot(spread.astype(jnp.bfloat16), move, preferred_element_type=jnp.float32)
    rows = 64.0 * total[:PLANE] + total[PLANE:]
    for d in range(PLANE):
        packed[d] = rows[d : d + 1]
    index_in[0] = packed[me.spot]
    for dy, dz in FAR_FIRST:
        spot, target = me.on_plane(dy, dz)
        remote(packed.at[spot], index_in.at[dy * NZ + dz], meta_plane, 0, target).start()

    near_vis(1).wait_recv()
    forward(1)

    others = sky.at[pl.ds(0, PLANE - 1)]
    remote(others, others, sky_plane, 0, me.partner).wait_recv()
    for dx in (2, 1, 3):
        spread_x(dx).start()
    spread_pair(0).start()

    @pl.loop(2, NEAR)
    def _(i):
        near_vis(i).wait_recv()
        forward(i)

    for dx in (1, 3, 2):
        spread_x(dx).wait_recv()
        spread_pair(NX - dx).start()
    far_index = index_in.at[pl.ds(1, PLANE - 1)]
    remote(far_index, far_index, meta_plane, 0, me.partner).wait()
    index_out[...] = index_in[...].astype(jnp.int32)
    for dx in range(NX):
        spread_pair(dx).wait()
    sky_out[...] = sky[...]
    for dx in (1, 3, 2):
        spread_x(dx).wait_send()
    for i in range(1, NEAR):
        near_meta(i).wait_send()
        near_vis(i).wait_send()
    remote(others, others, sky_plane, 0, me.partner).wait_send()
    arrived = vis_in.at[pl.ds(1, PLANE - 1)]
    remote(arrived, arrived, vis_plane, 0, me.partner).wait()
    vis_out[...] = vis_in[...]


def exchange(start_piece, strips, visibilities):
    dma = pltpu.SemaphoreType.DMA
    vmem = pltpu.VMEM
    sky = (OWNERS, PIECE, STRIP)
    index = (PLANE, 1, STRIP)
    blocks = (PLANE, NEAR, 4, STRIP)
    return pl.pallas_call(
        exchange_kernel,
        out_shape=(
            jax.ShapeDtypeStruct(sky, jnp.bfloat16),
            jax.ShapeDtypeStruct(index, jnp.int32),
            jax.ShapeDtypeStruct(blocks, jnp.bfloat16),
        ),
        in_specs=[pl.BlockSpec(memory_space=vmem)] * 3,
        out_specs=(pl.BlockSpec(memory_space=vmem),) * 3,
        scratch_shapes=[
            vmem(sky, jnp.bfloat16),
            vmem((NEAR, NZ * 4, STRIP), jnp.int32),
            vmem(index, jnp.float32),
            vmem(index, jnp.float32),
            vmem((NEAR * PLANE, 4, STRIP), jnp.bfloat16),
            vmem(blocks, jnp.bfloat16),
            dma((2, 1)),
            dma((2, NX)),
            dma((2, NX)),
            dma((2, NEAR)),
            dma((2, 1)),
            dma((2, NEAR)),
            dma((2, 1)),
            dma((2,)),
        ],
        compiler_params=pltpu.CompilerParams(collective_id=2, has_side_effects=True),
        name="exchange",
    )(start_piece, strips, visibilities)


def gather_rows(index_smem, sky_ref, strips, picked):
    @pl.loop(0, OWNERS // 8)
    def _(i):
        block = sky_ref[pl.ds(i * 8, 8)].astype(jnp.float32)
        strips[pl.ds(pl.multiple_of(i * 64, 64), 64)] = block.reshape(64, STRIP)

    @pl.loop(0, PLANE)
    def _(k):
        for i in range(NEAR):
            for q in range(4):
                strip = index_smem[k, 0, 4 * i + q]
                picked[q, k, pl.ds(i, 1)] = strips[pl.ds(strip, 1)]


def back_projected(picked, vis_ref, kernel_ref, adjoint, adjoint_low):
    for ch in range(2):
        weights = kernel_ref[ch, 0]
        gathered = jnp.concatenate(
            [picked[2 * ch + j].reshape(BLOCKS, STRIP).astype(jnp.bfloat16) for j in range(TERMS)], axis=1
        )
        predicted = jnp.dot(gathered, weights, preferred_element_type=jnp.float32)
        observed = vis_ref[ch].astype(jnp.float32)
        residual = jnp.where(observed < FLAGGED, predicted - observed, 0.0).astype(jnp.bfloat16)
        back = lax.dot_general(residual, weights, (((1,), (1,)), ((), ())), preferred_element_type=jnp.float32)
        for j in range(TERMS):
            adjoint[pl.ds(2 * ch + j, BLOCKS, stride=4)] = back[:, j * STRIP : (j + 1) * STRIP]

    @pl.loop(0, READS // 128)
    def _(i):
        rows = pl.ds(pl.multiple_of(i * 128, 128), 128)
        adjoint_low[rows] = adjoint[rows].astype(jnp.bfloat16)


def selectors(index_ref, high_rows, low_hits):
    group = lax.broadcasted_iota(jnp.int32, (1, STRIP), 1) // GROUP
    row = lax.broadcasted_iota(jnp.int32, (HALF, STRIP), 0)
    for m in range(READS // STRIP):
        number = index_ref[4 * m]
        for part in range(1, 4):
            number = jnp.where(group == part, index_ref[4 * m + part], number)
        high = number // HALF
        high_rows[m] = jnp.broadcast_to(high, (16, STRIP))
        low = jnp.broadcast_to(number - high * HALF, (HALF, STRIP))
        low_hits[:, m * STRIP : (m + 1) * STRIP] = jnp.where(low == row, 1.0, 0.0).astype(jnp.bfloat16)


def scatter_block(block, high_rows, low_hits, hits, adjoint_low):
    for h in range(PLANE * PIECE // HALF):
        for m in range(READS // STRIP):
            lanes = slice(m * STRIP, (m + 1) * STRIP)
            here = jnp.where(high_rows[m] == block * (PLANE * PIECE // HALF) + h, 1.0, 0.0).astype(jnp.bfloat16)
            here = jnp.concatenate([here] * (HALF // 16), axis=0)
            hits[h * HALF : (h + 1) * HALF, lanes] = here * low_hits[:, lanes]
    return jnp.dot(hits[...], adjoint_low[...], preferred_element_type=jnp.float32)


def iterate_kernel(
    final,
    step_size,
    index_smem,
    index_ref,
    sky_ref,
    vis_ref,
    kernel_ref,
    est_ref,
    out_ref,
    est_out,
    strips,
    picked,
    adjoint,
    adjoint_low,
    high_rows,
    low_hits,
    hits,
    image,
    got1,
    sum1,
    got2,
    sum2,
    got3,
    sky,
    sems1,
    sems2,
    sems3,
    sems4,
    sems5,
    sems6,
):
    me = Place()
    targets = [me.on_plane(dy, dz)[1] for dy, dz in FAR_FIRST]
    if final:
        targets += [me.on_chan(dy, dx) for dy, dx in CHAN_FAR_FIRST if dy and dx]
    wait_for_all = greet(targets + [me.on_x(dx) for dx in (2, 1, 3)] + [me.partner])

    def own_block(xx):
        return pl.ds((me.core * NX + xx) * PLANE, PLANE)

    def pair_copy(dx):
        block = image.at[pl.ds(((1 - me.core) * NX + lax.rem(me.x + dx, NX)) * PLANE, PLANE)]
        return remote(block, got1.at[dx], sems1, dx, me.partner)

    def x_copy(dx):
        target = (me.y * NX + lax.rem(me.x + dx, NX), me.facet)
        return remote(sum1.at[dx], got2.at[dx], sems2, dx, target)

    gather_rows(index_smem, sky_ref, strips, picked)
    back_projected(picked, vis_ref, kernel_ref, adjoint, adjoint_low)
    selectors(index_ref, high_rows, low_hits)

    @pl.loop(0, 2 * NX)
    def _(t):
        dx = lax.rem(t + 1, NX)
        core = jnp.where(t < NX, 1 - me.core, me.core)
        block = core * NX + lax.rem(me.x + dx, NX)
        part = scatter_block(block, high_rows, low_hits, hits, adjoint_low)
        image[pl.ds(block * PLANE, PLANE)] = part.reshape(PLANE, PIECE, STRIP).astype(jnp.bfloat16)

        @pl.when(t == NX - 1)
        def _():
            wait_for_all()
            for first in (1, 2, 3, 0):
                pair_copy(first).start()

        @pl.when(jnp.logical_and(t >= NX, t < 2 * NX - 1))
        def _():
            pair_copy(dx).wait_recv()
            for i in range(PLANE // 8):
                mine = image[pl.ds(block * PLANE + i * 8, 8)].astype(jnp.float32)
                total = mine + got1[dx, pl.ds(i * 8, 8)].astype(jnp.float32)
                sum1[dx, pl.ds(i * 8, 8)] = total.astype(jnp.bfloat16)
            x_copy(dx).start()

    order = [1, 2, 3, 0]
    pair_copy(0).wait_recv()
    for dx in order[:-1]:
        x_copy(dx).wait_recv()
    base = me.owner * PLANE

    @pl.loop(0, PLANE // 8)
    def _(i):
        rows = pl.ds(i * 8, 8)
        total = image[pl.ds(base + i * 8, 8)].astype(jnp.float32) + got1[0, rows].astype(jnp.float32)
        for dx in order[:-1]:
            total += got2[dx, rows].astype(jnp.float32)
        sum2[rows] = total.astype(jnp.bfloat16)

    for dy, dz in FAR_FIRST:
        place, target = me.on_plane(dy, dz)
        remote(sum2.at[place], got3.at[dy * NZ + dz], sems3, 0, target).start()
    others = got3.at[pl.ds(1, PLANE - 1)]
    all_plane = remote(others, others, sems3, 0, me.partner)
    all_plane.wait_recv()

    parts = [sum2[me.spot].astype(jnp.float32)] + [jnp.zeros((PIECE, STRIP), jnp.float32) for _ in range(3)]
    for k in range(1, PLANE):
        parts[k % 4] += got3[k].astype(jnp.float32)
    gradient = (parts[0] + parts[1]) + (parts[2] + parts[3])
    estimate = jnp.maximum(est_ref[...] - step_size * gradient - shrinkage, 0.0)

    if final:
        mine = sky.at[pl.ds(pl.multiple_of(me.chan * PIECE, PIECE), PIECE)]
        mine[...] = estimate
        for dy, dx in CHAN_FAR_FIRST:
            remote(mine, mine, sems4, 0, me.on_chan(dy, dx)).start()
        est_out[...] = estimate
        rest = sky.at[pl.ds(0, (NY * NX - 1) * PIECE)]
        remote(rest, rest, sems4, 0, me.partner).wait()
        for quarter in range(4):
            out_ref[:, quarter * STRIP : (quarter + 1) * STRIP] = sky[pl.ds(quarter, 2 * NY * NX, stride=4)]
    else:
        mine = sky.at[me.owner * PLANE + me.spot]
        mine[...] = estimate.astype(jnp.bfloat16)
        for dy, dz in FAR_FIRST:
            remote(mine, mine, sems4, 0, me.on_plane(dy, dz)[1]).start()
        est_out[...] = estimate
        rest = sky.at[pl.ds(0, PLANE - 1)]
        all_sky = remote(rest, rest, sems4, 0, me.partner)
        all_sky.wait_recv()

        def spread_x(dx):
            block = sky.at[own_block(me.x)]
            return remote(block, block, sems5, dx, me.on_x(dx))

        def spread_pair(dx):
            block = sky.at[own_block(me.xs[dx])]
            return remote(block, block, sems6, dx, me.partner)

        for dx in (2, 1, 3):
            spread_x(dx).start()
        spread_pair(0).start()
        for dx in order[:-1]:
            spread_x(dx).wait_recv()
            spread_pair(NX - dx).start()
        for dx in range(NX):
            spread_pair(dx).wait()
        out_ref[...] = sky[...]
        for dx in order[:-1]:
            spread_x(dx).wait_send()
        all_sky.wait_send()

    for dx in order:
        pair_copy(dx).wait_send()
    for dx in order[:-1]:
        x_copy(dx).wait_send()
    all_plane.wait_send()


def iterate(final, step_size, index, sky_now, visibilities, kernels, estimate):
    def body(*refs):
        iterate_kernel(final, step_size, *refs)

    dma = pltpu.SemaphoreType.DMA
    vmem = pltpu.VMEM
    blocks = (NX, PLANE, PIECE, STRIP)
    if final:
        out = jax.ShapeDtypeStruct((2 * NY * NX, 4 * STRIP), jnp.float32)
        sky = vmem((NY * NX * PIECE, STRIP), jnp.float32)
    else:
        out = jax.ShapeDtypeStruct((OWNERS, PIECE, STRIP), jnp.bfloat16)
        sky = vmem(out.shape, out.dtype)
    return pl.pallas_call(
        body,
        out_shape=(out, jax.ShapeDtypeStruct((PIECE, STRIP), jnp.float32)),
        in_specs=[pl.BlockSpec(memory_space=pltpu.SMEM)] + [pl.BlockSpec(memory_space=vmem)] * 5,
        out_specs=(pl.BlockSpec(memory_space=vmem),) * 2,
        scratch_shapes=[
            vmem((OWNERS * PIECE, STRIP), jnp.float32),
            vmem((4, PLANE, NEAR, STRIP), jnp.float32),
            vmem((READS, STRIP), jnp.float32),
            vmem((READS, STRIP), jnp.bfloat16),
            vmem((READS // STRIP, 16, STRIP), jnp.int32),
            vmem((HALF, READS), jnp.bfloat16),
            vmem((PLANE * PIECE, READS), jnp.bfloat16),
            vmem((OWNERS, PIECE, STRIP), jnp.bfloat16),
            vmem(blocks, jnp.bfloat16),
            vmem(blocks, jnp.bfloat16),
            vmem(blocks, jnp.bfloat16),
            vmem(blocks[1:], jnp.bfloat16),
            vmem(blocks[1:], jnp.bfloat16),
            sky,
            dma((2, NX)),
            dma((2, NX)),
            dma((2, 1)),
            dma((2, 1)),
            dma((2, NX)),
            dma((2, NX)),
        ],
        compiler_params=pltpu.CompilerParams(collective_id=1 if final else 0, has_side_effects=True),
        name="iterate_final" if final else "iterate_sky",
    )(index, index, sky_now, visibilities, kernels, estimate)


def owner_order(strip):
    quarter = strip % 4
    core = strip // 4 % 2
    z = strip // 8 % 8
    low_row = strip // 64 % 2
    x = strip // 128 % 4
    y = strip // 512
    return (((core * NX + x) * NY + y) * NZ + z) * PIECE + low_row * 4 + quarter


def on_device(start_image, visibilities, strip_index, live_counts, uv_kernels):
    slot_count = lax.axis_size("chan") * lax.axis_size("facet")
    channels, uvtiles = visibilities.shape[1:3]
    slab_rows, facet_width = start_image.shape
    strip_count = OWNERS * PIECE
    step_size = strip_count / (2.5 * slot_count * channels * uvtiles)

    lane_ids = jnp.arange(2 * VISB, dtype=jnp.int32) % VISB
    live_mask = lane_ids < live_counts[..., None]
    marked = jnp.where(live_mask, visibilities, jnp.bfloat16(FLAGGED))
    marked = marked.reshape(NY, NX, 2, NZ, 2, 2, STRIP).transpose(4, 1, 0, 3, 2, 5, 6)
    strips = owner_order(strip_index).transpose(0, 2, 3, 1).reshape(NZ * 4, channels)
    strips = jnp.pad(strips, ((0, 0), (0, STRIP - channels)))
    rows = lax.dynamic_slice_in_dim(start_image, lax.axis_index("chan") * 2, 2, 0)
    estimate = rows.reshape(PIECE, STRIP)
    sky, picked, observed = exchange(
        estimate.astype(jnp.bfloat16),
        strips,
        marked.reshape(OWNERS, 4, STRIP),
    )
    observed = observed.reshape(slot_count, 2, 2 * VISB).swapaxes(0, 1)
    for iteration in range(ITERS):
        sky, estimate = iterate(iteration == ITERS - 1, step_size, picked, sky, observed, uv_kernels, estimate)
    return sky


def solution(mesh):
    placed = (
        P(None, "facet"),
        P(("chan", "facet"), None, None, None),
        P(("chan", "facet"), None, None, None),
        P(("chan", "facet"), None, None),
        P("chan", "facet", None, None),
    )
    return jax.shard_map(
        on_device, mesh=mesh, in_specs=placed, out_specs=P(None, "facet"), check_vma=False
    )
```

```python
import jax
import jax.numpy as jnp
from jax import lax
from jax.experimental import pallas as pl
from jax.experimental.pallas import tpu as pltpu
from jax.sharding import PartitionSpec as P

STRIP = 128
VISB = 128
TERMS = 2
ITERS = 2
NX = 4
NY = 8
NZ = 8
PLANE = NY * NZ
OWNERS = 2 * NX * PLANE
PIECE = 8
NEAR = 2 * NX
GROUP = 4 * NEAR
BLOCKS = PLANE * NEAR
READS = 4 * BLOCKS
HALF = 64

FLAGGED = 1024.0

shrinkage = 0.05
MESH = pl.DeviceIdType.MESH


class Place:
    def __init__(self):
        chan = lax.axis_index("chan")
        facet = lax.axis_index("facet")
        self.chan, self.facet = chan, facet
        self.y, self.x = chan // NX, chan % NX
        self.z, self.core = facet // 2, facet % 2
        self.spot = self.y * NZ + self.z
        self.owner = self.core * NX + self.x
        self.ys = [lax.rem(self.y + d, NY) for d in range(NY)]
        self.zs = [lax.rem(self.z + d, NZ) for d in range(NZ)]
        self.xs = [lax.rem(self.x + d, NX) for d in range(NX)]
        self.chan_y = [yy * NX + self.x for yy in self.ys]
        self.facet_z = [zz * 2 + self.core for zz in self.zs]
        self.partner = (chan, self.z * 2 + (1 - self.core))

    def on_x(self, dx):
        return (self.y * NX + self.xs[dx], self.facet)

    def on_plane(self, dy, dz):
        return self.ys[dy] * NZ + self.zs[dz], (self.chan_y[dy], self.facet_z[dz])

    def on_chan(self, dy, dx):
        return (self.ys[dy] * NX + self.xs[dx], self.facet)

    def near(self, i):
        core = lax.rem(self.core + lax.rem(i, 2), 2)
        step = i // 2
        xx = lax.rem(self.x + step * (step + 1) // 2, NX)
        return core * NX + xx, (self.y * NX + xx, self.z * 2 + core)


def reach(d, length):
    return min(d, length - d)


FAR_FIRST = sorted(
    ((dy, dz) for dy in range(NY) for dz in range(NZ) if dy or dz),
    key=lambda step: -reach(step[0], NY) - reach(step[1], NZ),
)
CHAN_FAR_FIRST = sorted(
    ((dy, dx) for dy in range(NY) for dx in range(NX) if dy or dx),
    key=lambda step: -reach(step[0], NY) - reach(step[1], NX),
)


def remote(src, dst, sems, at, target):
    return pltpu.make_async_remote_copy(
        src_ref=src,
        dst_ref=dst,
        send_sem=sems.at[0, at],
        recv_sem=sems.at[1, at],
        device_id=target,
        device_id_type=MESH,
    )


def greet(targets):
    barrier = pltpu.get_barrier_semaphore()
    for target in targets:
        pl.semaphore_signal(barrier, inc=1, device_id=target, device_id_type=MESH)
    return lambda: pl.semaphore_wait(barrier, len(targets))


def owner_order(strip):
    quarter = strip % 4
    core = strip // 4 % 2
    z = strip // 8 % 8
    low_row = strip // 64 % 2
    x = strip // 128 % 4
    y = strip // 512
    return (((core * NX + x) * NY + y) * NZ + z) * PIECE + low_row * 4 + quarter


def gather_rows(index_smem, sky_ref, strips, picked):
    @pl.loop(0, OWNERS // 8)
    def _(i):
        block = sky_ref[pl.ds(i * 8, 8)].astype(jnp.float32)
        strips[pl.ds(pl.multiple_of(i * 64, 64), 64)] = block.reshape(64, STRIP)

    @pl.loop(0, PLANE)
    def _(k):
        for i in range(NEAR):
            for q in range(4):
                strip = index_smem[k, 0, 4 * i + q]
                picked[q, k, pl.ds(i, 1)] = strips[pl.ds(strip, 1)]


def selectors(index_ref, high_rows, low_hits):
    group = lax.broadcasted_iota(jnp.int32, (1, STRIP), 1) // GROUP
    row = lax.broadcasted_iota(jnp.int32, (HALF, STRIP), 0)
    for m in range(READS // STRIP):
        number = index_ref[4 * m]
        for part in range(1, 4):
            number = jnp.where(group == part, index_ref[4 * m + part], number)
        high = number // HALF
        high_rows[m] = jnp.broadcast_to(high, (16, STRIP))
        low = jnp.broadcast_to(number - high * HALF, (HALF, STRIP))
        low_hits[:, m * STRIP : (m + 1) * STRIP] = jnp.where(low == row, 1.0, 0.0).astype(jnp.bfloat16)


def scatter_block(block, high_rows, low_hits, hits, adjoint_low):
    for h in range(PLANE * PIECE // HALF):
        for m in range(READS // STRIP):
            lanes = slice(m * STRIP, (m + 1) * STRIP)
            here = jnp.where(high_rows[m] == block * (PLANE * PIECE // HALF) + h, 1.0, 0.0).astype(jnp.bfloat16)
            here = jnp.concatenate([here] * (HALF // 16), axis=0)
            hits[h * HALF : (h + 1) * HALF, lanes] = here * low_hits[:, lanes]
    return jnp.dot(hits[...], adjoint_low[...], preferred_element_type=jnp.float32)


class Named:
    def __init__(self, names, refs):
        for name, ref in zip(names, refs):
            setattr(self, name, ref)


def scratch_shapes():
    vmem = pltpu.VMEM
    dma = pltpu.SemaphoreType.DMA
    low, wide, whole = jnp.bfloat16, jnp.float32, jnp.int32
    blocks = (NX, PLANE, PIECE, STRIP)
    index = (PLANE, 1, STRIP)
    shapes = dict(
        estimate=vmem((PIECE, STRIP), wide),
        start=vmem((PIECE, STRIP), low),
        numbers=vmem((NZ * 4, STRIP), whole),
        near_numbers=vmem((NEAR, NZ * 4, STRIP), whole),
        packed=vmem(index, wide),
        index_in=vmem(index, wide),
        index_now=vmem(index, whole),
        index_smem=pltpu.SMEM(index, whole),
        mixed=vmem((4 * 2 * NZ, STRIP), wide),
        vis_send=vmem((OWNERS, 4, STRIP), low),
        vis_near=vmem((NEAR * PLANE, 4, STRIP), low),
        vis_in=vmem((PLANE, NEAR, 4, STRIP), low),
        observed=vmem((READS, STRIP), wide),
        strips=vmem((OWNERS * PIECE, STRIP), wide),
        picked=vmem((4, PLANE, NEAR, STRIP), wide),
        adjoint=vmem((READS, STRIP), wide),
        adjoint_low=vmem((READS, STRIP), low),
        high_rows=vmem((READS // STRIP, 16, STRIP), whole),
        low_hits=vmem((HALF, READS), low),
        hits=vmem((PLANE * PIECE, READS), low),
        image=vmem((OWNERS, PIECE, STRIP), low),
        final_image=vmem((NY * NX * PIECE, STRIP), wide),
        to_chan=dma((2, 1)),
        to_meta_near=dma((2, NEAR)),
        to_meta_plane=dma((2, 1)),
        to_vis_near=dma((2, NEAR)),
        to_vis_plane=dma((2, 1)),
        local=dma((2,)),
    )
    for it in range(ITERS):
        shapes.update(
            {
                f"sky{it}": vmem((OWNERS, PIECE, STRIP), low),
                f"to_sky_plane{it}": dma((2, 1)),
                f"to_sky_x{it}": dma((2, NX)),
                f"to_sky_pair{it}": dma((2, NX)),
                f"got_pair{it}": vmem(blocks, low),
                f"sum_pair{it}": vmem(blocks, low),
                f"got_x{it}": vmem(blocks, low),
                f"sum_x{it}": vmem(blocks[1:], low),
                f"got_plane{it}": vmem(blocks[1:], low),
                f"to_pair{it}": dma((2, NX)),
                f"to_x{it}": dma((2, NX)),
                f"to_plane{it}": dma((2, 1)),
            }
        )
    return shapes


def of_iteration(s, it):
    names = [name[:-1] for name in vars(s) if name.endswith(str(it))]
    return Named(names, [getattr(s, name + str(it)) for name in names])


def prepare(me, s, start_ref, index_ref, counts_ref, vis_ref):
    for quarter in range(4):
        columns = slice(quarter * STRIP, (quarter + 1) * STRIP)
        s.mixed[:8] = start_ref[pl.ds(pl.multiple_of(me.chan // 4 * 8, 8), 8), columns]
        for low in range(2):
            s.estimate[4 * low + quarter : 4 * low + quarter + 1] = s.mixed[pl.ds(me.chan % 4 * 2 + low, 1)]
    s.start[...] = s.estimate[...].astype(jnp.bfloat16)
    s.sky0[me.owner * PLANE + me.spot] = s.estimate[...].astype(jnp.bfloat16)
    channels = index_ref.shape[1]
    s.numbers[...] = jnp.zeros(s.numbers.shape, jnp.int32)
    s.numbers[:, :channels] = owner_order(index_ref[...])
    lane = lax.broadcasted_iota(jnp.int32, (2 * NZ, STRIP), 1)
    for y in range(NY):
        for x in range(NX):
            for ch in range(2):
                chan = (y * NX + x) * 2 + ch
                live = lane < counts_ref[:, chan : chan + 1]
                for half in range(2):
                    block = vis_ref[chan, :, half * STRIP : (half + 1) * STRIP].astype(jnp.float32)
                    s.mixed[pl.ds(ch * 2 + half, 2 * NZ, stride=4)] = jnp.where(live, block, FLAGGED)
            for z in range(NZ):
                for core in range(2):
                    row = (z * 2 + core) * 4
                    owner = ((core * NX + x) * NY + y) * NZ + z
                    s.vis_send[owner] = s.mixed[row : row + 4].astype(jnp.bfloat16)


def spread_sky_plane(me, sky, sems, source):
    own = sky.at[me.owner * PLANE + me.spot]
    for dy, dz in FAR_FIRST:
        remote(own if source is None else source, own, sems, 0, me.on_plane(dy, dz)[1]).start()
    others = sky.at[pl.ds(0, PLANE - 1)]
    return remote(others, others, sems, 0, me.partner)


def sky_spreaders(me, t):
    def own_block(dx):
        return t.sky.at[pl.ds((me.core * NX + me.xs[dx]) * PLANE, PLANE)]

    def spread_x(dx):
        return remote(own_block(0), own_block(0), t.to_sky_x, dx, me.on_x(dx))

    def spread_pair(dx):
        return remote(own_block(dx), own_block(dx), t.to_sky_pair, dx, me.partner)

    return spread_x, spread_pair


def pack_numbers(me, s):
    lane = lax.broadcasted_iota(jnp.int32, (PLANE, STRIP), 1)
    place = lax.broadcasted_iota(jnp.int32, (PLANE, STRIP), 0)
    belongs = (lane // 2) == (place // NZ) * NX + me.x
    column = lax.broadcasted_iota(jnp.int32, (STRIP, STRIP), 1)
    source = lax.broadcasted_iota(jnp.int32, (STRIP, STRIP), 0)
    total = jnp.zeros((2 * PLANE, STRIP), jnp.float32)
    for i in range(NEAR):
        held = s.numbers if i == 0 else s.near_numbers.at[i]
        for j in range(TERMS):
            strips = held[pl.ds(me.core * 2 + j, NZ, stride=4)]
            high = strips // 64
            low = strips - 64 * high
            spread = jnp.concatenate(
                [
                    jnp.where(belongs, jnp.concatenate([part.astype(jnp.float32)] * NY, axis=0), 0.0)
                    for part in (high, low)
                ],
                axis=0,
            )
            move = jnp.where(column % GROUP == 4 * i + 2 * (source % 2) + j, 1.0, 0.0).astype(jnp.bfloat16)
            total += jnp.dot(spread.astype(jnp.bfloat16), move, preferred_element_type=jnp.float32)
    rows = 64.0 * total[:PLANE] + total[PLANE:]
    for d in range(PLANE):
        s.packed[d] = rows[d : d + 1]
    s.index_in[0] = s.packed[me.spot]


def exchange(me, s):
    t = of_iteration(s, 0)
    own_vis = pltpu.make_async_copy(
        s.vis_send.at[pl.ds(me.owner * PLANE, PLANE)], s.vis_near.at[pl.ds(0, PLANE)], s.local.at[0]
    )
    own_vis.start()
    all_sky = spread_sky_plane(me, t.sky, t.to_sky_plane, s.start)
    spread_x, spread_pair = sky_spreaders(me, t)

    def near_meta(i):
        return remote(s.numbers, s.near_numbers.at[i], s.to_meta_near, i, me.near(i)[1])

    def near_vis(i):
        owner, target = me.near(i)
        block = s.vis_send.at[pl.ds(owner * PLANE, PLANE)]
        return remote(block, s.vis_near.at[pl.ds(i * PLANE, PLANE)], s.to_vis_near, i, target)

    for i in range(1, NEAR):
        near_meta(i).start()
    for i in range(1, NEAR):
        near_vis(i).start()
    own_vis.wait()

    def forward(i):
        base = i * PLANE
        s.vis_in[0, i] = s.vis_near[base + me.spot]
        for dy, dz in FAR_FIRST:
            place, target = me.on_plane(dy, dz)
            remote(s.vis_near.at[base + place], s.vis_in.at[dy * NZ + dz, i], s.to_vis_plane, 0, target).start()

    forward(0)
    for i in range(1, NEAR):
        near_meta(i).wait_recv()
    pack_numbers(me, s)
    for dy, dz in FAR_FIRST:
        spot, target = me.on_plane(dy, dz)
        remote(s.packed.at[spot], s.index_in.at[dy * NZ + dz], s.to_meta_plane, 0, target).start()
    near_vis(1).wait_recv()
    forward(1)
    all_sky.wait_recv()
    for dx in (2, 1, 3):
        spread_x(dx).start()
    spread_pair(0).start()

    @pl.loop(2, NEAR)
    def _(i):
        near_vis(i).wait_recv()
        forward(i)

    far_index = s.index_in.at[pl.ds(1, PLANE - 1)]
    all_index = remote(far_index, far_index, s.to_meta_plane, 0, me.partner)
    all_index.wait_recv()
    s.index_now[...] = jnp.clip(s.index_in[...].astype(jnp.int32), 0, OWNERS * PIECE - 1)
    to_smem = pltpu.make_async_copy(s.index_now, s.index_smem, s.local.at[1])
    to_smem.start()
    selectors(s.index_now, s.high_rows, s.low_hits)
    for dx in (1, 3, 2):
        spread_x(dx).wait_recv()
        spread_pair(NX - dx).start()
    to_smem.wait()
    for dx in range(NX):
        spread_pair(dx).wait_recv()
    gather_rows(s.index_smem, t.sky, s.strips, s.picked)

    arrived = s.vis_in.at[pl.ds(1, PLANE - 1)]
    all_vis = remote(arrived, arrived, s.to_vis_plane, 0, me.partner)
    all_vis.wait_recv()

    @pl.loop(0, PLANE)
    def _(k):
        rows = pl.ds(pl.multiple_of(k * 4 * NEAR, 4 * NEAR), 4 * NEAR)
        s.observed[rows] = s.vis_in[k].astype(jnp.float32).reshape(4 * NEAR, STRIP)

    def finish():
        all_index.wait_send()
        all_vis.wait_send()
        all_sky.wait_send()
        for dx in range(1, NX):
            spread_x(dx).wait_send()
        for dx in range(NX):
            spread_pair(dx).wait_send()
        for i in range(1, NEAR):
            near_meta(i).wait_send()
            near_vis(i).wait_send()

    return finish


def back_projected(s, kernel_ref):
    for ch in range(2):
        weights = kernel_ref[ch, 0]
        gathered = jnp.concatenate(
            [s.picked[2 * ch + j].reshape(BLOCKS, STRIP).astype(jnp.bfloat16) for j in range(TERMS)], axis=1
        )
        predicted = jnp.dot(gathered, weights, preferred_element_type=jnp.float32)
        halves = []
        for half in range(2):
            observed = s.observed[pl.ds(2 * ch + half, BLOCKS, stride=4)]
            model = predicted[:, half * STRIP : (half + 1) * STRIP]
            halves.append(jnp.where(observed < FLAGGED, model - observed, 0.0).astype(jnp.bfloat16))
        residual = jnp.concatenate(halves, axis=1)
        back = lax.dot_general(residual, weights, (((1,), (1,)), ((), ())), preferred_element_type=jnp.float32)
        for j in range(TERMS):
            s.adjoint[pl.ds(2 * ch + j, BLOCKS, stride=4)] = back[:, j * STRIP : (j + 1) * STRIP]

    @pl.loop(0, READS // 128)
    def _(i):
        rows = pl.ds(pl.multiple_of(i * 128, 128), 128)
        s.adjoint_low[rows] = s.adjoint[rows].astype(jnp.bfloat16)


def reduce_gradient(me, s, it):
    t = of_iteration(s, it)

    def pair_copy(dx):
        block = s.image.at[pl.ds(((1 - me.core) * NX + lax.rem(me.x + dx, NX)) * PLANE, PLANE)]
        return remote(block, t.got_pair.at[dx], t.to_pair, dx, me.partner)

    def x_copy(dx):
        target = (me.y * NX + lax.rem(me.x + dx, NX), me.facet)
        return remote(t.sum_pair.at[dx], t.got_x.at[dx], t.to_x, dx, target)

    @pl.loop(0, 2 * NX)
    def _(step):
        dx = lax.rem(step + 1, NX)
        core = jnp.where(step < NX, 1 - me.core, me.core)
        block = core * NX + lax.rem(me.x + dx, NX)
        part = scatter_block(block, s.high_rows, s.low_hits, s.hits, s.adjoint_low)
        s.image[pl.ds(block * PLANE, PLANE)] = part.reshape(PLANE, PIECE, STRIP).astype(jnp.bfloat16)

        @pl.when(step < NX)
        def _():
            pair_copy(dx).start()

        @pl.when(jnp.logical_and(step >= NX, step < 2 * NX - 1))
        def _():
            pair_copy(dx).wait_recv()
            for i in range(PLANE // 8):
                mine = s.image[pl.ds(block * PLANE + i * 8, 8)].astype(jnp.float32)
                total = mine + t.got_pair[dx, pl.ds(i * 8, 8)].astype(jnp.float32)
                t.sum_pair[dx, pl.ds(i * 8, 8)] = total.astype(jnp.bfloat16)
            x_copy(dx).start()

    pair_copy(0).wait_recv()
    for dx in range(1, NX):
        x_copy(dx).wait_recv()

    @pl.loop(0, PLANE // 8)
    def _(i):
        rows = pl.ds(i * 8, 8)
        total = s.image[pl.ds(me.owner * PLANE + i * 8, 8)].astype(jnp.float32) + t.got_pair[0, rows].astype(jnp.float32)
        for dx in range(1, NX):
            total += t.got_x[dx, rows].astype(jnp.float32)
        t.sum_x[rows] = total.astype(jnp.bfloat16)

    for dy, dz in FAR_FIRST:
        place, target = me.on_plane(dy, dz)
        remote(t.sum_x.at[place], t.got_plane.at[dy * NZ + dz], t.to_plane, 0, target).start()
    others = t.got_plane.at[pl.ds(1, PLANE - 1)]
    all_plane = remote(others, others, t.to_plane, 0, me.partner)
    all_plane.wait_recv()
    parts = [t.sum_x[me.spot].astype(jnp.float32)] + [jnp.zeros((PIECE, STRIP), jnp.float32) for _ in range(3)]
    for k in range(1, PLANE):
        parts[k % 4] += t.got_plane[k].astype(jnp.float32)

    def finish():
        for dx in range(NX):
            pair_copy(dx).wait_send()
        for dx in range(1, NX):
            x_copy(dx).wait_send()
        all_plane.wait_send()

    return (parts[0] + parts[1]) + (parts[2] + parts[3]), finish


def reconstruct_kernel(step_size, names, start_ref, index_ref, counts_ref, vis_ref, kernel_ref, out_ref, *scratch):
    s = Named(names, scratch)
    me = Place()
    wait_for_all = greet(
        [me.on_plane(dy, dz)[1] for dy, dz in FAR_FIRST]
        + [me.on_chan(dy, dx) for dy, dx in CHAN_FAR_FIRST if dy and dx]
        + [me.near(i)[1] for i in range(1, NEAR)]
    )
    prepare(me, s, start_ref, index_ref, counts_ref, vis_ref)
    wait_for_all()
    waits = [exchange(me, s)]
    for it in range(ITERS):
        if it:
            gather_rows(s.index_smem, getattr(s, f"sky{it}"), s.strips, s.picked)
        back_projected(s, kernel_ref)
        gradient, finish = reduce_gradient(me, s, it)
        estimate = jnp.maximum(s.estimate[...] - step_size * gradient - shrinkage, 0.0)
        if it == ITERS - 1:
            mine = s.final_image.at[pl.ds(pl.multiple_of(me.chan * PIECE, PIECE), PIECE)]
            mine[...] = estimate
            for dy, dx in CHAN_FAR_FIRST:
                remote(mine, mine, s.to_chan, 0, me.on_chan(dy, dx)).start()
            rest = s.final_image.at[pl.ds(0, (NY * NX - 1) * PIECE)]
            remote(rest, rest, s.to_chan, 0, me.partner).wait()
            for quarter in range(4):
                columns = slice(quarter * STRIP, (quarter + 1) * STRIP)
                out_ref[:, columns] = s.final_image[pl.ds(quarter, 2 * NY * NX, stride=4)]
            waits.append(finish)
        else:
            t = of_iteration(s, it + 1)
            t.sky[me.owner * PLANE + me.spot] = estimate.astype(jnp.bfloat16)
            all_sky = spread_sky_plane(me, t.sky, t.to_sky_plane, None)
            s.estimate[...] = estimate
            finish()
            spread_x, spread_pair = sky_spreaders(me, t)
            all_sky.wait_recv()
            for dx in (2, 1, 3):
                spread_x(dx).start()
            spread_pair(0).start()
            for dx in (1, 3, 2):
                spread_x(dx).wait_recv()
                spread_pair(NX - dx).start()
            for dx in range(NX):
                spread_pair(dx).wait()
            for dx in range(1, NX):
                spread_x(dx).wait_send()
            all_sky.wait_send()
    for finish in waits:
        finish()


def on_device(start_image, visibilities, strip_index, live_counts, uv_kernels):
    slot_count = lax.axis_size("chan") * lax.axis_size("facet")
    channels, uvtiles = visibilities.shape[1:3]
    step_size = OWNERS * PIECE / (2.5 * slot_count * channels * uvtiles)
    strips = strip_index.transpose(0, 2, 3, 1).reshape(uvtiles * TERMS, channels)
    counts = live_counts.transpose(0, 2, 1).reshape(uvtiles, channels)
    shapes = scratch_shapes()

    def body(*refs):
        reconstruct_kernel(step_size, list(shapes), *refs)

    return pl.pallas_call(
        body,
        out_shape=jax.ShapeDtypeStruct(start_image.shape, jnp.float32),
        in_specs=[pl.BlockSpec(memory_space=pltpu.VMEM)] * 5,
        out_specs=pl.BlockSpec(memory_space=pltpu.VMEM),
        scratch_shapes=list(shapes.values()),
        compiler_params=pltpu.CompilerParams(collective_id=0, has_side_effects=True),
        name="reconstruct",
    )(start_image, strips, counts, visibilities[0], uv_kernels)


def solution(mesh):
    placed = (
        P(None, "facet"),
        P(("chan", "facet"), None, None, None),
        P(("chan", "facet"), None, None, None),
        P(("chan", "facet"), None, None),
        P("chan", "facet", None, None),
    )
    return jax.shard_map(
        on_device, mesh=mesh, in_specs=placed, out_specs=P(None, "facet"), check_vma=False
    )
```

```python
import jax
import jax.numpy as jnp
from jax import lax
from jax.experimental import pallas as pl
from jax.experimental.pallas import tpu as pltpu
from jax.sharding import PartitionSpec as P

STRIP = 128
VISB = 128
TERMS = 2
ITERS = 2
NX = 4
NY = 8
NZ = 8
PLANE = NY * NZ
OWNERS = 2 * NX * PLANE
PIECE = 8
NEAR = 2 * NX
GROUP = 4 * NEAR
BLOCKS = PLANE * NEAR
READS = 4 * BLOCKS
HALF = 64

FLAGGED = 1024.0

shrinkage = 0.05
MESH = pl.DeviceIdType.MESH


class Place:
    def __init__(self):
        chan = lax.axis_index("chan")
        facet = lax.axis_index("facet")
        self.chan, self.facet = chan, facet
        self.y, self.x = chan // NX, chan % NX
        self.z, self.core = facet // 2, facet % 2
        self.spot = self.y * NZ + self.z
        self.owner = self.core * NX + self.x
        self.ys = [lax.rem(self.y + d, NY) for d in range(NY)]
        self.zs = [lax.rem(self.z + d, NZ) for d in range(NZ)]
        self.xs = [lax.rem(self.x + d, NX) for d in range(NX)]
        self.chan_y = [yy * NX + self.x for yy in self.ys]
        self.facet_z = [zz * 2 + self.core for zz in self.zs]
        self.partner = (chan, self.z * 2 + (1 - self.core))

    def on_x(self, dx):
        return (self.y * NX + self.xs[dx], self.facet)

    def on_plane(self, dy, dz):
        return self.ys[dy] * NZ + self.zs[dz], (self.chan_y[dy], self.facet_z[dz])

    def on_chan(self, dy, dx):
        return (self.ys[dy] * NX + self.xs[dx], self.facet)

    def near(self, i):
        core = lax.rem(self.core + lax.rem(i, 2), 2)
        step = i // 2
        xx = lax.rem(self.x + step * (step + 1) // 2, NX)
        return core * NX + xx, (self.y * NX + xx, self.z * 2 + core)


def reach(d, length):
    return min(d, length - d)


FAR_FIRST = sorted(
    ((dy, dz) for dy in range(NY) for dz in range(NZ) if dy or dz),
    key=lambda step: -reach(step[0], NY) - reach(step[1], NZ),
)
CHAN_FAR_FIRST = sorted(
    ((dy, dx) for dy in range(NY) for dx in range(NX) if dy or dx),
    key=lambda step: -reach(step[0], NY) - reach(step[1], NX),
)


ROWS_NEAR = sorted(range(NY), key=lambda d: reach(d, NY))
ROWS_FAR = ROWS_NEAR[::-1]
COLUMNS_FAR = sorted(range(NZ), key=lambda d: -reach(d, NZ))
BLOCK_STEPS = ((2, 0), (1, 0), (2, 1), (3, 0), (1, 1), (3, 1), (0, 0), (0, 1))


def pick(step, values):
    value = values[0]
    for at, other in enumerate(values[1:], 1):
        value = jnp.where(step == at, other, value)
    return value


def remote(src, dst, sems, at, target):
    return pltpu.make_async_remote_copy(
        src_ref=src,
        dst_ref=dst,
        send_sem=sems.at[0, at],
        recv_sem=sems.at[1, at],
        device_id=target,
        device_id_type=MESH,
    )


def greet(targets):
    barrier = pltpu.get_barrier_semaphore()
    for target in targets:
        pl.semaphore_signal(barrier, inc=1, device_id=target, device_id_type=MESH)
    return lambda: pl.semaphore_wait(barrier, len(targets))


def owner_order(strip):
    quarter = strip % 4
    core = strip // 4 % 2
    z = strip // 8 % 8
    low_row = strip // 64 % 2
    x = strip // 128 % 4
    y = strip // 512
    return (((core * NX + x) * NY + y) * NZ + z) * PIECE + low_row * 4 + quarter


def gather_rows(index_smem, sky_ref, strips, picked):
    @pl.loop(0, OWNERS // 8)
    def _(i):
        block = sky_ref[pl.ds(i * 8, 8)].astype(jnp.float32)
        strips[pl.ds(pl.multiple_of(i * 64, 64), 64)] = block.reshape(64, STRIP)

    @pl.loop(0, PLANE)
    def _(k):
        for i in range(NEAR):
            for q in range(4):
                strip = index_smem[k, 0, 4 * i + q]
                picked[q, k, pl.ds(i, 1)] = strips[pl.ds(strip, 1)]


def selectors(index_ref, high_rows, low_hits):
    group = lax.broadcasted_iota(jnp.int32, (1, STRIP), 1) // GROUP
    row = lax.broadcasted_iota(jnp.int32, (HALF, STRIP), 0)
    for m in range(READS // STRIP):
        number = index_ref[4 * m]
        for part in range(1, 4):
            number = jnp.where(group == part, index_ref[4 * m + part], number)
        high = number // HALF
        high_rows[m] = jnp.broadcast_to(high, (16, STRIP))
        low = jnp.broadcast_to(number - high * HALF, (HALF, STRIP))
        low_hits[:, m * STRIP : (m + 1) * STRIP] = jnp.where(low == row, 1.0, 0.0).astype(jnp.bfloat16)


def scatter_block(block, high_rows, low_hits, hits, adjoint_low):
    for h in range(PLANE * PIECE // HALF):
        for m in range(READS // STRIP):
            lanes = slice(m * STRIP, (m + 1) * STRIP)
            here = jnp.where(high_rows[m] == block * (PLANE * PIECE // HALF) + h, 1.0, 0.0).astype(jnp.bfloat16)
            here = jnp.concatenate([here] * (HALF // 16), axis=0)
            hits[h * HALF : (h + 1) * HALF, lanes] = here * low_hits[:, lanes]
    return jnp.dot(hits[...], adjoint_low[...], preferred_element_type=jnp.float32)


class Named:
    def __init__(self, names, refs):
        for name, ref in zip(names, refs):
            setattr(self, name, ref)


def scratch_shapes():
    vmem = pltpu.VMEM
    dma = pltpu.SemaphoreType.DMA
    low, wide, whole = jnp.bfloat16, jnp.float32, jnp.int32
    blocks = (NX, PLANE, PIECE, STRIP)
    index = (PLANE, 1, STRIP)
    shapes = dict(
        estimate=vmem((PIECE, STRIP), wide),
        start=vmem((PIECE, STRIP), low),
        numbers=vmem((NZ * 4, STRIP), whole),
        near_numbers=vmem((NEAR, NZ * 4, STRIP), whole),
        packed=vmem(index, wide),
        index_in=vmem(index, wide),
        index_now=vmem(index, whole),
        index_smem=pltpu.SMEM(index, whole),
        mixed=vmem((4 * 2 * NZ, STRIP), wide),
        vis_send=vmem((OWNERS, 4, STRIP), low),
        vis_near=vmem((NEAR * PLANE, 4, STRIP), low),
        vis_in=vmem((PLANE, NEAR, 4, STRIP), low),
        observed=vmem((READS, STRIP), wide),
        strips=vmem((OWNERS * PIECE, STRIP), wide),
        picked=vmem((4, PLANE, NEAR, STRIP), wide),
        adjoint=vmem((READS, STRIP), wide),
        adjoint_low=vmem((READS, STRIP), low),
        high_rows=vmem((READS // STRIP, 16, STRIP), whole),
        low_hits=vmem((HALF, READS), low),
        hits=vmem((PLANE * PIECE, READS), low),
        image=vmem((OWNERS, PIECE, STRIP), low),
        final_image=vmem((NY * NX * PIECE, STRIP), wide),
        to_chan=dma((2, 1)),
        to_meta_near=dma((2, NEAR)),
        to_meta_plane=dma((2, 1)),
        to_vis_near=dma((2, NEAR)),
        to_vis_plane=dma((2, 1)),
        local=dma((2,)),
    )
    for it in range(ITERS):
        shapes.update(
            {
                f"sky{it}": vmem((OWNERS, PIECE, STRIP), low),
                f"to_sky_plane{it}": dma((2, NY)),
                f"to_sky_x{it}": dma((2, NX * NY)),
                f"to_sky_pair{it}": dma((2, NX)),
                f"got_pair{it}": vmem(blocks, low),
                f"sum_pair{it}": vmem(blocks, low),
                f"got_x{it}": vmem(blocks, low),
                f"sum_x{it}": vmem(blocks[1:], low),
                f"got_plane{it}": vmem(blocks[1:], low),
                f"to_pair{it}": dma((2, NX)),
                f"to_x{it}": dma((2, NX * NY)),
                f"to_plane{it}": dma((2, 1)),
            }
        )
    return shapes


def of_iteration(s, it):
    names = [name[:-1] for name in vars(s) if name.endswith(str(it))]
    return Named(names, [getattr(s, name + str(it)) for name in names])


def prepare(me, s, start_ref, index_ref, counts_ref, vis_ref):
    for quarter in range(4):
        columns = slice(quarter * STRIP, (quarter + 1) * STRIP)
        s.mixed[:8] = start_ref[pl.ds(pl.multiple_of(me.chan // 4 * 8, 8), 8), columns]
        for low in range(2):
            s.estimate[4 * low + quarter : 4 * low + quarter + 1] = s.mixed[pl.ds(me.chan % 4 * 2 + low, 1)]
    s.start[...] = s.estimate[...].astype(jnp.bfloat16)
    s.sky0[me.owner * PLANE + me.spot] = s.estimate[...].astype(jnp.bfloat16)
    channels = index_ref.shape[1]
    s.numbers[...] = jnp.zeros(s.numbers.shape, jnp.int32)
    s.numbers[:, :channels] = owner_order(index_ref[...])
    lane = lax.broadcasted_iota(jnp.int32, (2 * NZ, STRIP), 1)
    for y in range(NY):
        for x in range(NX):
            for ch in range(2):
                chan = (y * NX + x) * 2 + ch
                live = lane < counts_ref[:, chan : chan + 1]
                for half in range(2):
                    block = vis_ref[chan, :, half * STRIP : (half + 1) * STRIP].astype(jnp.float32)
                    s.mixed[pl.ds(ch * 2 + half, 2 * NZ, stride=4)] = jnp.where(live, block, FLAGGED)
            for z in range(NZ):
                for core in range(2):
                    row = (z * 2 + core) * 4
                    owner = ((core * NX + x) * NY + y) * NZ + z
                    s.vis_send[owner] = s.mixed[row : row + 4].astype(jnp.bfloat16)


class SkySpread:
    def __init__(self, me, t, source=None):
        self.me, self.t = me, t
        own = t.sky.at[me.owner * PLANE + me.spot]
        for dy, dz in FAR_FIRST:
            remote(own if source is None else source, own, t.to_sky_plane, dy, me.on_plane(dy, dz)[1]).start()

    def row(self, dx, dy):
        me = self.me
        return self.t.sky.at[pl.ds(((me.core * NX + me.xs[dx]) * NY + me.ys[-dy % NY]) * NZ, NZ)]

    def plane(self, dy):
        rows = self.t.sky.at[pl.ds(self.me.owner * PLANE, NZ - 1)] if dy == 0 else self.row(0, dy)
        return remote(rows, rows, self.t.to_sky_plane, dy, self.me.partner)

    def across(self, dx, dy):
        row = self.row(0, dy)
        return remote(row, row, self.t.to_sky_x, dx * NY + dy, self.me.on_x(dx))

    def pair(self, dx, dy):
        row = self.row(dx, dy)
        return remote(row, row, self.t.to_sky_pair, dx, self.me.partner)

    def whole_pair(self, dx):
        block = self.t.sky.at[pl.ds((self.me.core * NX + self.me.xs[dx]) * PLANE, PLANE)]
        return remote(block, block, self.t.to_sky_pair, dx, self.me.partner)

    def pass_rows(self):
        for dy in ROWS_NEAR:
            self.plane(dy).wait_recv()
            for dx in (2, 1, 3):
                self.across(dx, dy).start()
            self.pair(0, dy).start()

    def pass_blocks(self):
        for dy in ROWS_NEAR:
            for dx in (1, 3, 2):
                self.across(dx, dy).wait_recv()
                self.pair(NX - dx, dy).start()

    def arrived(self):
        for dx in range(NX):
            self.whole_pair(dx).wait_recv()

    def finish(self):
        for dy in range(NY):
            self.plane(dy).wait_send()
            for dx in range(1, NX):
                self.across(dx, dy).wait_send()
        for dx in range(NX):
            self.whole_pair(dx).wait_send()


def pack_numbers(me, s):
    lane = lax.broadcasted_iota(jnp.int32, (PLANE, STRIP), 1)
    place = lax.broadcasted_iota(jnp.int32, (PLANE, STRIP), 0)
    belongs = (lane // 2) == (place // NZ) * NX + me.x
    column = lax.broadcasted_iota(jnp.int32, (STRIP, STRIP), 1)
    source = lax.broadcasted_iota(jnp.int32, (STRIP, STRIP), 0)
    total = jnp.zeros((2 * PLANE, STRIP), jnp.float32)
    for i in range(NEAR):
        held = s.numbers if i == 0 else s.near_numbers.at[i]
        for j in range(TERMS):
            strips = held[pl.ds(me.core * 2 + j, NZ, stride=4)]
            high = strips // 64
            low = strips - 64 * high
            spread = jnp.concatenate(
                [
                    jnp.where(belongs, jnp.concatenate([part.astype(jnp.float32)] * NY, axis=0), 0.0)
                    for part in (high, low)
                ],
                axis=0,
            )
            move = jnp.where(column % GROUP == 4 * i + 2 * (source % 2) + j, 1.0, 0.0).astype(jnp.bfloat16)
            total += jnp.dot(spread.astype(jnp.bfloat16), move, preferred_element_type=jnp.float32)
    rows = 64.0 * total[:PLANE] + total[PLANE:]
    for d in range(PLANE):
        s.packed[d] = rows[d : d + 1]
    s.index_in[0] = s.packed[me.spot]


def exchange(me, s):
    t = of_iteration(s, 0)
    own_vis = pltpu.make_async_copy(
        s.vis_send.at[pl.ds(me.owner * PLANE, PLANE)], s.vis_near.at[pl.ds(0, PLANE)], s.local.at[0]
    )
    own_vis.start()
    spread = SkySpread(me, t, s.start)

    def near_meta(i):
        return remote(s.numbers, s.near_numbers.at[i], s.to_meta_near, i, me.near(i)[1])

    def near_vis(i):
        owner, target = me.near(i)
        block = s.vis_send.at[pl.ds(owner * PLANE, PLANE)]
        return remote(block, s.vis_near.at[pl.ds(i * PLANE, PLANE)], s.to_vis_near, i, target)

    for i in range(1, NEAR):
        near_meta(i).start()
    for i in range(1, NEAR):
        near_vis(i).start()
    own_vis.wait()

    def forward(i):
        base = i * PLANE
        s.vis_in[0, i] = s.vis_near[base + me.spot]
        for dy, dz in FAR_FIRST:
            place, target = me.on_plane(dy, dz)
            remote(s.vis_near.at[base + place], s.vis_in.at[dy * NZ + dz, i], s.to_vis_plane, 0, target).start()

    forward(0)
    for i in range(1, NEAR):
        near_meta(i).wait_recv()
    pack_numbers(me, s)
    for dy, dz in FAR_FIRST:
        spot, target = me.on_plane(dy, dz)
        remote(s.packed.at[spot], s.index_in.at[dy * NZ + dz], s.to_meta_plane, 0, target).start()
    near_vis(1).wait_recv()
    forward(1)
    spread.pass_rows()

    @pl.loop(2, NEAR)
    def _(i):
        near_vis(i).wait_recv()
        forward(i)

    far_index = s.index_in.at[pl.ds(1, PLANE - 1)]
    all_index = remote(far_index, far_index, s.to_meta_plane, 0, me.partner)
    all_index.wait_recv()
    s.index_now[...] = jnp.clip(s.index_in[...].astype(jnp.int32), 0, OWNERS * PIECE - 1)
    to_smem = pltpu.make_async_copy(s.index_now, s.index_smem, s.local.at[1])
    to_smem.start()
    selectors(s.index_now, s.high_rows, s.low_hits)
    spread.pass_blocks()
    to_smem.wait()
    spread.arrived()
    gather_rows(s.index_smem, t.sky, s.strips, s.picked)

    arrived = s.vis_in.at[pl.ds(1, PLANE - 1)]
    all_vis = remote(arrived, arrived, s.to_vis_plane, 0, me.partner)
    all_vis.wait_recv()

    @pl.loop(0, PLANE)
    def _(k):
        rows = pl.ds(pl.multiple_of(k * 4 * NEAR, 4 * NEAR), 4 * NEAR)
        s.observed[rows] = s.vis_in[k].astype(jnp.float32).reshape(4 * NEAR, STRIP)

    def finish():
        all_index.wait_send()
        all_vis.wait_send()
        spread.finish()
        for i in range(1, NEAR):
            near_meta(i).wait_send()
            near_vis(i).wait_send()

    return finish


def back_projected(s, kernel_ref):
    for ch in range(2):
        weights = kernel_ref[ch, 0]
        gathered = jnp.concatenate(
            [s.picked[2 * ch + j].reshape(BLOCKS, STRIP).astype(jnp.bfloat16) for j in range(TERMS)], axis=1
        )
        predicted = jnp.dot(gathered, weights, preferred_element_type=jnp.float32)
        halves = []
        for half in range(2):
            observed = s.observed[pl.ds(2 * ch + half, BLOCKS, stride=4)]
            model = predicted[:, half * STRIP : (half + 1) * STRIP]
            halves.append(jnp.where(observed < FLAGGED, model - observed, 0.0).astype(jnp.bfloat16))
        residual = jnp.concatenate(halves, axis=1)
        back = lax.dot_general(residual, weights, (((1,), (1,)), ((), ())), preferred_element_type=jnp.float32)
        for j in range(TERMS):
            s.adjoint[pl.ds(2 * ch + j, BLOCKS, stride=4)] = back[:, j * STRIP : (j + 1) * STRIP]

    @pl.loop(0, READS // 128)
    def _(i):
        rows = pl.ds(pl.multiple_of(i * 128, 128), 128)
        s.adjoint_low[rows] = s.adjoint[rows].astype(jnp.bfloat16)


def reduce_gradient(me, s, it):
    t = of_iteration(s, it)

    def pair_copy(dx):
        block = s.image.at[pl.ds(((1 - me.core) * NX + lax.rem(me.x + dx, NX)) * PLANE, PLANE)]
        return remote(block, t.got_pair.at[dx], t.to_pair, dx, me.partner)

    def x_copy(dx, dy):
        target = (me.y * NX + lax.rem(me.x + dx, NX), me.facet)
        row = pl.ds(me.ys[dy] * NZ, NZ)
        return remote(t.sum_pair.at[dx, row], t.got_x.at[dx, row], t.to_x, dx * NY + dy, target)

    @pl.loop(0, 2 * NX)
    def _(step):
        dx = pick(step, [shift for shift, _ in BLOCK_STEPS])
        own = pick(step, [mine for _, mine in BLOCK_STEPS])
        core = lax.rem(me.core + 1 + own, 2)
        block = core * NX + lax.rem(me.x + dx, NX)
        part = scatter_block(block, s.high_rows, s.low_hits, s.hits, s.adjoint_low)
        s.image[pl.ds(block * PLANE, PLANE)] = part.reshape(PLANE, PIECE, STRIP).astype(jnp.bfloat16)

        @pl.when(own == 0)
        def _():
            pair_copy(dx).start()

        @pl.when(jnp.logical_and(own == 1, dx > 0))
        def _():
            pair_copy(dx).wait_recv()
            for dy in ROWS_FAR:
                row = pl.ds(me.ys[dy] * NZ, NZ)
                mine = s.image[pl.ds(block * PLANE + me.ys[dy] * NZ, NZ)].astype(jnp.float32)
                t.sum_pair[dx, row] = (mine + t.got_pair[dx, row].astype(jnp.float32)).astype(jnp.bfloat16)
                x_copy(dx, dy).start()

    pair_copy(0).wait_recv()
    for dy in ROWS_FAR:
        row = pl.ds(me.ys[dy] * NZ, NZ)
        total = s.image[pl.ds(me.owner * PLANE + me.ys[dy] * NZ, NZ)].astype(jnp.float32)
        total += t.got_pair[0, row].astype(jnp.float32)
        for dx in (2, 1, 3):
            x_copy(dx, dy).wait_recv()
            total += t.got_x[dx, row].astype(jnp.float32)
        t.sum_x[row] = total.astype(jnp.bfloat16)
        for dz in COLUMNS_FAR:
            if dy or dz:
                place, target = me.on_plane(dy, dz)
                remote(t.sum_x.at[place], t.got_plane.at[dy * NZ + dz], t.to_plane, 0, target).start()
    others = t.got_plane.at[pl.ds(1, PLANE - 1)]
    all_plane = remote(others, others, t.to_plane, 0, me.partner)
    all_plane.wait_recv()
    parts = [t.sum_x[me.spot].astype(jnp.float32)] + [jnp.zeros((PIECE, STRIP), jnp.float32) for _ in range(3)]
    for k in range(1, PLANE):
        parts[k % 4] += t.got_plane[k].astype(jnp.float32)

    def finish():
        for dx in range(NX):
            pair_copy(dx).wait_send()
        for dx in range(1, NX):
            for dy in range(NY):
                x_copy(dx, dy).wait_send()
        all_plane.wait_send()

    return (parts[0] + parts[1]) + (parts[2] + parts[3]), finish


def reconstruct_kernel(step_size, names, start_ref, index_ref, counts_ref, vis_ref, kernel_ref, out_ref, *scratch):
    s = Named(names, scratch)
    me = Place()
    wait_for_all = greet(
        [me.on_plane(dy, dz)[1] for dy, dz in FAR_FIRST]
        + [me.on_chan(dy, dx) for dy, dx in CHAN_FAR_FIRST if dy and dx]
        + [me.near(i)[1] for i in range(1, NEAR)]
    )
    prepare(me, s, start_ref, index_ref, counts_ref, vis_ref)
    wait_for_all()
    waits = [exchange(me, s)]
    for it in range(ITERS):
        if it:
            gather_rows(s.index_smem, getattr(s, f"sky{it}"), s.strips, s.picked)
        back_projected(s, kernel_ref)
        gradient, finish = reduce_gradient(me, s, it)
        estimate = jnp.maximum(s.estimate[...] - step_size * gradient - shrinkage, 0.0)
        if it == ITERS - 1:
            mine = s.final_image.at[pl.ds(pl.multiple_of(me.chan * PIECE, PIECE), PIECE)]
            mine[...] = estimate
            for dy, dx in CHAN_FAR_FIRST:
                remote(mine, mine, s.to_chan, 0, me.on_chan(dy, dx)).start()
            rest = s.final_image.at[pl.ds(0, (NY * NX - 1) * PIECE)]
            remote(rest, rest, s.to_chan, 0, me.partner).wait()
            for quarter in range(4):
                columns = slice(quarter * STRIP, (quarter + 1) * STRIP)
                out_ref[:, columns] = s.final_image[pl.ds(quarter, 2 * NY * NX, stride=4)]
            waits.append(finish)
        else:
            t = of_iteration(s, it + 1)
            t.sky[me.owner * PLANE + me.spot] = estimate.astype(jnp.bfloat16)
            spread = SkySpread(me, t)
            s.estimate[...] = estimate
            finish()
            spread.pass_rows()
            spread.pass_blocks()
            spread.arrived()
            waits.append(spread.finish)
    for finish in waits:
        finish()


def on_device(start_image, visibilities, strip_index, live_counts, uv_kernels):
    slot_count = lax.axis_size("chan") * lax.axis_size("facet")
    channels, uvtiles = visibilities.shape[1:3]
    step_size = OWNERS * PIECE / (2.5 * slot_count * channels * uvtiles)
    strips = strip_index.transpose(0, 2, 3, 1).reshape(uvtiles * TERMS, channels)
    counts = live_counts.transpose(0, 2, 1).reshape(uvtiles, channels)
    shapes = scratch_shapes()

    def body(*refs):
        reconstruct_kernel(step_size, list(shapes), *refs)

    return pl.pallas_call(
        body,
        out_shape=jax.ShapeDtypeStruct(start_image.shape, jnp.float32),
        in_specs=[pl.BlockSpec(memory_space=pltpu.VMEM)] * 5,
        out_specs=pl.BlockSpec(memory_space=pltpu.VMEM),
        scratch_shapes=list(shapes.values()),
        compiler_params=pltpu.CompilerParams(collective_id=0, has_side_effects=True),
        name="reconstruct",
    )(start_image, strips, counts, visibilities[0], uv_kernels)


def solution(mesh):
    placed = (
        P(None, "facet"),
        P(("chan", "facet"), None, None, None),
        P(("chan", "facet"), None, None, None),
        P(("chan", "facet"), None, None),
        P("chan", "facet", None, None),
    )
    return jax.shard_map(
        on_device, mesh=mesh, in_specs=placed, out_specs=P(None, "facet"), check_vma=False
    )
```

```python
import jax
import jax.numpy as jnp
from jax import lax
from jax.experimental import pallas as pl
from jax.experimental.pallas import tpu as pltpu
from jax.sharding import PartitionSpec as P

STRIP = 128
VISB = 128
TERMS = 2
ITERS = 2
NX = 4
NY = 8
NZ = 8
PLANE = NY * NZ
OWNERS = 2 * NX * PLANE
PIECE = 8
NEAR = 2 * NX
GROUP = 4 * NEAR
BLOCKS = PLANE * NEAR
READS = 4 * BLOCKS
HALF = 64

FLAGGED = 1024.0

shrinkage = 0.05
MESH = pl.DeviceIdType.MESH


class Place:
    def __init__(self):
        chan = lax.axis_index("chan")
        facet = lax.axis_index("facet")
        self.chan, self.facet = chan, facet
        self.y, self.x = chan // NX, chan % NX
        self.z, self.core = facet // 2, facet % 2
        self.spot = self.y * NZ + self.z
        self.owner = self.core * NX + self.x
        self.ys = [lax.rem(self.y + d, NY) for d in range(NY)]
        self.zs = [lax.rem(self.z + d, NZ) for d in range(NZ)]
        self.xs = [lax.rem(self.x + d, NX) for d in range(NX)]
        self.chan_y = [yy * NX + self.x for yy in self.ys]
        self.facet_z = [zz * 2 + self.core for zz in self.zs]
        self.partner = (chan, self.z * 2 + (1 - self.core))

    def on_x(self, dx):
        return (self.y * NX + self.xs[dx], self.facet)

    def on_plane(self, dy, dz):
        return self.ys[dy] * NZ + self.zs[dz], (self.chan_y[dy], self.facet_z[dz])

    def on_chan(self, dy, dx):
        return (self.ys[dy] * NX + self.xs[dx], self.facet)

    def near(self, i):
        core = lax.rem(self.core + lax.rem(i, 2), 2)
        step = i // 2
        xx = lax.rem(self.x + step * (step + 1) // 2, NX)
        return core * NX + xx, (self.y * NX + xx, self.z * 2 + core)


def reach(d, length):
    return min(d, length - d)


FAR_FIRST = sorted(
    ((dy, dz) for dy in range(NY) for dz in range(NZ) if dy or dz),
    key=lambda step: -reach(step[0], NY) - reach(step[1], NZ),
)
CHAN_FAR_FIRST = sorted(
    ((dy, dx) for dy in range(NY) for dx in range(NX) if dy or dx),
    key=lambda step: -reach(step[0], NY) - reach(step[1], NX),
)


ROWS_NEAR = sorted(range(NY), key=lambda d: reach(d, NY))
ROWS_FAR = ROWS_NEAR[::-1]
COLUMNS_FAR = sorted(range(NZ), key=lambda d: -reach(d, NZ))
BLOCK_STEPS = ((2, 0), (1, 0), (2, 1), (3, 0), (1, 1), (3, 1), (0, 0), (0, 1))


def pick(step, values):
    value = values[0]
    for at, other in enumerate(values[1:], 1):
        value = jnp.where(step == at, other, value)
    return value


def remote(src, dst, sems, at, target):
    return pltpu.make_async_remote_copy(
        src_ref=src,
        dst_ref=dst,
        send_sem=sems.at[0, at],
        recv_sem=sems.at[1, at],
        device_id=target,
        device_id_type=MESH,
    )


def greet(targets):
    barrier = pltpu.get_barrier_semaphore()
    for target in targets:
        pl.semaphore_signal(barrier, inc=1, device_id=target, device_id_type=MESH)
    return lambda: pl.semaphore_wait(barrier, len(targets))


def owner_order(strip):
    quarter = strip % 4
    core = strip // 4 % 2
    z = strip // 8 % 8
    low_row = strip // 64 % 2
    x = strip // 128 % 4
    y = strip // 512
    return (((core * NX + x) * NY + y) * NZ + z) * PIECE + low_row * 4 + quarter


def gather_rows(index_smem, sky_ref, strips, picked):
    @pl.loop(0, OWNERS // 8)
    def _(i):
        block = sky_ref[pl.ds(i * 8, 8)].astype(jnp.float32)
        strips[pl.ds(pl.multiple_of(i * 64, 64), 64)] = block.reshape(64, STRIP)

    @pl.loop(0, PLANE)
    def _(k):
        for i in range(NEAR):
            for q in range(4):
                strip = index_smem[k, 0, 4 * i + q]
                picked[q, k, pl.ds(i, 1)] = strips[pl.ds(strip, 1)]


def selectors(index_ref, high_rows, low_hits):
    group = lax.broadcasted_iota(jnp.int32, (1, STRIP), 1) // GROUP
    row = lax.broadcasted_iota(jnp.int32, (HALF, STRIP), 0)
    for m in range(READS // STRIP):
        number = index_ref[4 * m]
        for part in range(1, 4):
            number = jnp.where(group == part, index_ref[4 * m + part], number)
        high = number // HALF
        high_rows[m] = jnp.broadcast_to(high, (16, STRIP))
        low = jnp.broadcast_to(number - high * HALF, (HALF, STRIP))
        low_hits[:, m * STRIP : (m + 1) * STRIP] = jnp.where(low == row, 1.0, 0.0).astype(jnp.bfloat16)


def scatter_block(block, high_rows, low_hits, hits, adjoint_low):
    for h in range(PLANE * PIECE // HALF):
        for m in range(READS // STRIP):
            lanes = slice(m * STRIP, (m + 1) * STRIP)
            here = jnp.where(high_rows[m] == block * (PLANE * PIECE // HALF) + h, 1.0, 0.0).astype(jnp.bfloat16)
            here = jnp.concatenate([here] * (HALF // 16), axis=0)
            hits[h * HALF : (h + 1) * HALF, lanes] = here * low_hits[:, lanes]
    return jnp.dot(hits[...], adjoint_low[...], preferred_element_type=jnp.float32)


class Named:
    def __init__(self, names, refs):
        for name, ref in zip(names, refs):
            setattr(self, name, ref)


def scratch_shapes(vis_shape, kernel_shape):
    vmem = pltpu.VMEM
    dma = pltpu.SemaphoreType.DMA
    low, wide, whole = jnp.bfloat16, jnp.float32, jnp.int32
    blocks = (NX, PLANE, PIECE, STRIP)
    index = (PLANE, 1, STRIP)
    shapes = dict(
        estimate=vmem((PIECE, STRIP), wide),
        start=vmem((PIECE, STRIP), low),
        numbers=vmem((NZ * 4, STRIP), whole),
        near_numbers=vmem((NEAR, NZ * 4, STRIP), whole),
        packed=vmem(index, wide),
        index_in=vmem(index, wide),
        index_now=vmem(index, whole),
        index_smem=pltpu.SMEM(index, whole),
        mixed=vmem((4 * 2 * NZ, STRIP), wide),
        vis_send=vmem((OWNERS, 4, STRIP), low),
        vis_near=vmem((NEAR * PLANE, 4, STRIP), low),
        vis_in=vmem((PLANE, NEAR, 4, STRIP), low),
        observed=vmem((READS, STRIP), wide),
        strips=vmem((OWNERS * PIECE, STRIP), wide),
        picked=vmem((4, PLANE, NEAR, STRIP), wide),
        adjoint=vmem((READS, STRIP), wide),
        adjoint_low=vmem((READS, STRIP), low),
        high_rows=vmem((READS // STRIP, 16, STRIP), whole),
        low_hits=vmem((HALF, READS), low),
        hits=vmem((PLANE * PIECE, READS), low),
        image=vmem((OWNERS, PIECE, STRIP), low),
        final_image=vmem((NY * NX * PIECE, STRIP), wide),
        to_chan=dma((2, 1)),
        to_meta_near=dma((2, NEAR)),
        to_meta_plane=dma((2, 1)),
        to_vis_near=dma((2, NEAR)),
        to_vis_plane=dma((2, 1)),
        local=dma((5,)),
        vis_own=vmem(vis_shape, low),
        weights=vmem(kernel_shape, low),
        start_rows=vmem((8, 4 * STRIP), wide),
    )
    for it in range(ITERS):
        shapes.update(
            {
                f"sky{it}": vmem((OWNERS, PIECE, STRIP), low),
                f"to_sky_plane{it}": dma((2, NY)),
                f"to_sky_x{it}": dma((2, NX * NY)),
                f"to_sky_pair{it}": dma((2, NX)),
                f"got_pair{it}": vmem(blocks, low),
                f"sum_pair{it}": vmem(blocks, low),
                f"got_x{it}": vmem(blocks, low),
                f"sum_x{it}": vmem(blocks[1:], low),
                f"got_plane{it}": vmem(blocks[1:], low),
                f"to_pair{it}": dma((2, NX)),
                f"to_x{it}": dma((2, NX * NY)),
                f"to_plane{it}": dma((2, 1)),
            }
        )
    return shapes


def of_iteration(s, it):
    names = [name[:-1] for name in vars(s) if name.endswith(str(it))]
    return Named(names, [getattr(s, name + str(it)) for name in names])


def prepare(me, s, index_ref, counts_ref):
    for quarter in range(4):
        columns = slice(quarter * STRIP, (quarter + 1) * STRIP)
        s.mixed[:8] = s.start_rows[:, columns]
        for low in range(2):
            s.estimate[4 * low + quarter : 4 * low + quarter + 1] = s.mixed[pl.ds(me.chan % 4 * 2 + low, 1)]
    s.start[...] = s.estimate[...].astype(jnp.bfloat16)
    s.sky0[me.owner * PLANE + me.spot] = s.estimate[...].astype(jnp.bfloat16)
    channels = index_ref.shape[1]
    s.numbers[...] = jnp.zeros(s.numbers.shape, jnp.int32)
    s.numbers[:, :channels] = owner_order(index_ref[...])
    lane = lax.broadcasted_iota(jnp.int32, (2 * NZ, STRIP), 1)
    for y in range(NY):
        for x in range(NX):
            for ch in range(2):
                chan = (y * NX + x) * 2 + ch
                live = lane < counts_ref[:, chan : chan + 1]
                for half in range(2):
                    block = s.vis_own[chan, :, half * STRIP : (half + 1) * STRIP].astype(jnp.float32)
                    s.mixed[pl.ds(ch * 2 + half, 2 * NZ, stride=4)] = jnp.where(live, block, FLAGGED)
            for z in range(NZ):
                for core in range(2):
                    row = (z * 2 + core) * 4
                    owner = ((core * NX + x) * NY + y) * NZ + z
                    s.vis_send[owner] = s.mixed[row : row + 4].astype(jnp.bfloat16)


class SkySpread:
    def __init__(self, me, t, source=None):
        self.me, self.t = me, t
        own = t.sky.at[me.owner * PLANE + me.spot]
        for dy, dz in FAR_FIRST:
            remote(own if source is None else source, own, t.to_sky_plane, dy, me.on_plane(dy, dz)[1]).start()

    def row(self, dx, dy):
        me = self.me
        return self.t.sky.at[pl.ds(((me.core * NX + me.xs[dx]) * NY + me.ys[-dy % NY]) * NZ, NZ)]

    def plane(self, dy):
        rows = self.t.sky.at[pl.ds(self.me.owner * PLANE, NZ - 1)] if dy == 0 else self.row(0, dy)
        return remote(rows, rows, self.t.to_sky_plane, dy, self.me.partner)

    def across(self, dx, dy):
        row = self.row(0, dy)
        return remote(row, row, self.t.to_sky_x, dx * NY + dy, self.me.on_x(dx))

    def pair(self, dx, dy):
        row = self.row(dx, dy)
        return remote(row, row, self.t.to_sky_pair, dx, self.me.partner)

    def whole_pair(self, dx):
        block = self.t.sky.at[pl.ds((self.me.core * NX + self.me.xs[dx]) * PLANE, PLANE)]
        return remote(block, block, self.t.to_sky_pair, dx, self.me.partner)

    def pass_rows(self):
        for dy in ROWS_NEAR:
            self.plane(dy).wait_recv()
            for dx in (2, 1, 3):
                self.across(dx, dy).start()
            self.pair(0, dy).start()

    def pass_blocks(self):
        for dy in ROWS_NEAR:
            for dx in (1, 3, 2):
                self.across(dx, dy).wait_recv()
                self.pair(NX - dx, dy).start()

    def arrived(self):
        for dx in range(NX):
            self.whole_pair(dx).wait_recv()

    def finish(self):
        for dy in range(NY):
            self.plane(dy).wait_send()
            for dx in range(1, NX):
                self.across(dx, dy).wait_send()
        for dx in range(NX):
            self.whole_pair(dx).wait_send()


def pack_numbers(me, s):
    lane = lax.broadcasted_iota(jnp.int32, (PLANE, STRIP), 1)
    place = lax.broadcasted_iota(jnp.int32, (PLANE, STRIP), 0)
    belongs = (lane // 2) == (place // NZ) * NX + me.x
    column = lax.broadcasted_iota(jnp.int32, (STRIP, STRIP), 1)
    source = lax.broadcasted_iota(jnp.int32, (STRIP, STRIP), 0)
    total = jnp.zeros((2 * PLANE, STRIP), jnp.float32)
    for i in range(NEAR):
        held = s.numbers if i == 0 else s.near_numbers.at[i]
        for j in range(TERMS):
            strips = held[pl.ds(me.core * 2 + j, NZ, stride=4)]
            high = strips // 64
            low = strips - 64 * high
            spread = jnp.concatenate(
                [
                    jnp.where(belongs, jnp.concatenate([part.astype(jnp.float32)] * NY, axis=0), 0.0)
                    for part in (high, low)
                ],
                axis=0,
            )
            move = jnp.where(column % GROUP == 4 * i + 2 * (source % 2) + j, 1.0, 0.0).astype(jnp.bfloat16)
            total += jnp.dot(spread.astype(jnp.bfloat16), move, preferred_element_type=jnp.float32)
    rows = 64.0 * total[:PLANE] + total[PLANE:]
    for d in range(PLANE):
        s.packed[d] = rows[d : d + 1]
    s.index_in[0] = s.packed[me.spot]


def exchange(me, s):
    t = of_iteration(s, 0)
    own_vis = pltpu.make_async_copy(
        s.vis_send.at[pl.ds(me.owner * PLANE, PLANE)], s.vis_near.at[pl.ds(0, PLANE)], s.local.at[0]
    )
    own_vis.start()

    def near_meta(i):
        return remote(s.numbers, s.near_numbers.at[i], s.to_meta_near, i, me.near(i)[1])

    def near_vis(i):
        owner, target = me.near(i)
        block = s.vis_send.at[pl.ds(owner * PLANE, PLANE)]
        return remote(block, s.vis_near.at[pl.ds(i * PLANE, PLANE)], s.to_vis_near, i, target)

    for i in range(1, NEAR):
        near_meta(i).start()
    for i in range(1, NEAR):
        near_vis(i).start()
    spread = SkySpread(me, t, s.start)
    own_vis.wait()

    def forward(i):
        base = i * PLANE
        s.vis_in[0, i] = s.vis_near[base + me.spot]
        for dy, dz in FAR_FIRST:
            place, target = me.on_plane(dy, dz)
            remote(s.vis_near.at[base + place], s.vis_in.at[dy * NZ + dz, i], s.to_vis_plane, 0, target).start()

    forward(0)
    for i in range(1, NEAR):
        near_meta(i).wait_recv()
    pack_numbers(me, s)
    for dy, dz in FAR_FIRST:
        spot, target = me.on_plane(dy, dz)
        remote(s.packed.at[spot], s.index_in.at[dy * NZ + dz], s.to_meta_plane, 0, target).start()
    @pl.loop(1, 6)
    def _(i):
        near_vis(i).wait_recv()
        forward(i)

    spread.pass_rows()

    @pl.loop(6, NEAR)
    def _(i):
        near_vis(i).wait_recv()
        forward(i)

    far_index = s.index_in.at[pl.ds(1, PLANE - 1)]
    all_index = remote(far_index, far_index, s.to_meta_plane, 0, me.partner)
    all_index.wait_recv()
    s.index_now[...] = jnp.clip(s.index_in[...].astype(jnp.int32), 0, OWNERS * PIECE - 1)
    to_smem = pltpu.make_async_copy(s.index_now, s.index_smem, s.local.at[1])
    to_smem.start()
    selectors(s.index_now, s.high_rows, s.low_hits)
    spread.pass_blocks()
    to_smem.wait()
    spread.arrived()
    gather_rows(s.index_smem, t.sky, s.strips, s.picked)

    arrived = s.vis_in.at[pl.ds(1, PLANE - 1)]
    all_vis = remote(arrived, arrived, s.to_vis_plane, 0, me.partner)
    all_vis.wait_recv()

    @pl.loop(0, PLANE)
    def _(k):
        rows = pl.ds(pl.multiple_of(k * 4 * NEAR, 4 * NEAR), 4 * NEAR)
        s.observed[rows] = s.vis_in[k].astype(jnp.float32).reshape(4 * NEAR, STRIP)

    def finish():
        all_index.wait_send()
        all_vis.wait_send()
        spread.finish()
        for i in range(1, NEAR):
            near_meta(i).wait_send()
            near_vis(i).wait_send()

    return finish


def back_projected(s, kernel_ref):
    for ch in range(2):
        weights = kernel_ref[ch, 0]
        gathered = jnp.concatenate(
            [s.picked[2 * ch + j].reshape(BLOCKS, STRIP).astype(jnp.bfloat16) for j in range(TERMS)], axis=1
        )
        predicted = jnp.dot(gathered, weights, preferred_element_type=jnp.float32)
        halves = []
        for half in range(2):
            observed = s.observed[pl.ds(2 * ch + half, BLOCKS, stride=4)]
            model = predicted[:, half * STRIP : (half + 1) * STRIP]
            halves.append(jnp.where(observed < FLAGGED, model - observed, 0.0).astype(jnp.bfloat16))
        residual = jnp.concatenate(halves, axis=1)
        back = lax.dot_general(residual, weights, (((1,), (1,)), ((), ())), preferred_element_type=jnp.float32)
        for j in range(TERMS):
            s.adjoint[pl.ds(2 * ch + j, BLOCKS, stride=4)] = back[:, j * STRIP : (j + 1) * STRIP]

    @pl.loop(0, READS // 128)
    def _(i):
        rows = pl.ds(pl.multiple_of(i * 128, 128), 128)
        s.adjoint_low[rows] = s.adjoint[rows].astype(jnp.bfloat16)


def reduce_gradient(me, s, it):
    t = of_iteration(s, it)

    def pair_copy(dx):
        block = s.image.at[pl.ds(((1 - me.core) * NX + lax.rem(me.x + dx, NX)) * PLANE, PLANE)]
        return remote(block, t.got_pair.at[dx], t.to_pair, dx, me.partner)

    def x_copy(dx, dy):
        target = (me.y * NX + lax.rem(me.x + dx, NX), me.facet)
        row = pl.ds(me.ys[dy] * NZ, NZ)
        return remote(t.sum_pair.at[dx, row], t.got_x.at[dx, row], t.to_x, dx * NY + dy, target)

    @pl.loop(0, 2 * NX)
    def _(step):
        dx = pick(step, [shift for shift, _ in BLOCK_STEPS])
        own = pick(step, [mine for _, mine in BLOCK_STEPS])
        core = lax.rem(me.core + 1 + own, 2)
        block = core * NX + lax.rem(me.x + dx, NX)
        part = scatter_block(block, s.high_rows, s.low_hits, s.hits, s.adjoint_low)
        s.image[pl.ds(block * PLANE, PLANE)] = part.reshape(PLANE, PIECE, STRIP).astype(jnp.bfloat16)

        @pl.when(own == 0)
        def _():
            pair_copy(dx).start()

        @pl.when(jnp.logical_and(own == 1, dx > 0))
        def _():
            pair_copy(dx).wait_recv()
            for dy in ROWS_FAR:
                row = pl.ds(me.ys[dy] * NZ, NZ)
                mine = s.image[pl.ds(block * PLANE + me.ys[dy] * NZ, NZ)].astype(jnp.float32)
                t.sum_pair[dx, row] = (mine + t.got_pair[dx, row].astype(jnp.float32)).astype(jnp.bfloat16)
                x_copy(dx, dy).start()

    pair_copy(0).wait_recv()
    for dy in ROWS_FAR:
        row = pl.ds(me.ys[dy] * NZ, NZ)
        total = s.image[pl.ds(me.owner * PLANE + me.ys[dy] * NZ, NZ)].astype(jnp.float32)
        total += t.got_pair[0, row].astype(jnp.float32)
        for dx in (2, 1, 3):
            x_copy(dx, dy).wait_recv()
            total += t.got_x[dx, row].astype(jnp.float32)
        t.sum_x[row] = total.astype(jnp.bfloat16)
        for dz in COLUMNS_FAR:
            if dy or dz:
                place, target = me.on_plane(dy, dz)
                remote(t.sum_x.at[place], t.got_plane.at[dy * NZ + dz], t.to_plane, 0, target).start()
    others = t.got_plane.at[pl.ds(1, PLANE - 1)]
    all_plane = remote(others, others, t.to_plane, 0, me.partner)
    all_plane.wait_recv()
    parts = [t.sum_x[me.spot].astype(jnp.float32)] + [jnp.zeros((PIECE, STRIP), jnp.float32) for _ in range(3)]
    for k in range(1, PLANE):
        parts[k % 4] += t.got_plane[k].astype(jnp.float32)

    def finish():
        for dx in range(NX):
            pair_copy(dx).wait_send()
        for dx in range(1, NX):
            for dy in range(NY):
                x_copy(dx, dy).wait_send()
        all_plane.wait_send()

    return (parts[0] + parts[1]) + (parts[2] + parts[3]), finish


def reconstruct_kernel(step_size, names, start_ref, index_ref, counts_ref, vis_ref, kernel_ref, out_ref, *scratch):
    s = Named(names, scratch)
    me = Place()
    rows = pl.ds(pl.multiple_of(me.chan // 4 * 8, 8), 8)
    loads = [
        pltpu.make_async_copy(source, target, s.local.at[2 + at])
        for at, (source, target) in enumerate(
            ((start_ref.at[rows], s.start_rows), (vis_ref, s.vis_own), (kernel_ref, s.weights))
        )
    ]
    for load in loads:
        load.start()
    wait_for_all = greet(
        [me.on_plane(dy, dz)[1] for dy, dz in FAR_FIRST]
        + [me.on_chan(dy, dx) for dy, dx in CHAN_FAR_FIRST if dy and dx]
        + [me.near(i)[1] for i in range(1, NEAR)]
    )
    for load in loads[:2]:
        load.wait()
    prepare(me, s, index_ref, counts_ref)
    wait_for_all()
    waits = [exchange(me, s)]
    for it in range(ITERS):
        if it:
            gather_rows(s.index_smem, getattr(s, f"sky{it}"), s.strips, s.picked)
        else:
            loads[2].wait()
        back_projected(s, s.weights)
        gradient, finish = reduce_gradient(me, s, it)
        estimate = jnp.maximum(s.estimate[...] - step_size * gradient - shrinkage, 0.0)
        if it == ITERS - 1:
            mine = s.final_image.at[pl.ds(pl.multiple_of(me.chan * PIECE, PIECE), PIECE)]
            mine[...] = estimate
            for dy, dx in CHAN_FAR_FIRST:
                remote(mine, mine, s.to_chan, 0, me.on_chan(dy, dx)).start()
            rest = s.final_image.at[pl.ds(0, (NY * NX - 1) * PIECE)]
            remote(rest, rest, s.to_chan, 0, me.partner).wait()
            for quarter in range(4):
                columns = slice(quarter * STRIP, (quarter + 1) * STRIP)
                out_ref[:, columns] = s.final_image[pl.ds(quarter, 2 * NY * NX, stride=4)]
            waits.append(finish)
        else:
            t = of_iteration(s, it + 1)
            t.sky[me.owner * PLANE + me.spot] = estimate.astype(jnp.bfloat16)
            spread = SkySpread(me, t)
            s.estimate[...] = estimate
            finish()
            spread.pass_rows()
            spread.pass_blocks()
            spread.arrived()
            waits.append(spread.finish)
    for finish in waits:
        finish()


def on_device(start_image, visibilities, strip_index, live_counts, uv_kernels):
    slot_count = lax.axis_size("chan") * lax.axis_size("facet")
    channels, uvtiles = visibilities.shape[1:3]
    step_size = OWNERS * PIECE / (2.5 * slot_count * channels * uvtiles)
    strips = strip_index.transpose(0, 2, 3, 1).reshape(uvtiles * TERMS, channels)
    counts = live_counts.transpose(0, 2, 1).reshape(uvtiles, channels)
    shapes = scratch_shapes(visibilities.shape[1:], uv_kernels.shape)

    def body(*refs):
        reconstruct_kernel(step_size, list(shapes), *refs)

    return pl.pallas_call(
        body,
        out_shape=jax.ShapeDtypeStruct(start_image.shape, jnp.float32),
        in_specs=[pl.BlockSpec(memory_space=space) for space in (pl.ANY, pltpu.VMEM, pltpu.VMEM, pl.ANY, pl.ANY)],
        out_specs=pl.BlockSpec(memory_space=pltpu.VMEM),
        scratch_shapes=list(shapes.values()),
        compiler_params=pltpu.CompilerParams(collective_id=0, has_side_effects=True),
        name="reconstruct",
    )(start_image, strips, counts, visibilities[0], uv_kernels)


def solution(mesh):
    placed = (
        P(None, "facet"),
        P(("chan", "facet"), None, None, None),
        P(("chan", "facet"), None, None, None),
        P(("chan", "facet"), None, None),
        P("chan", "facet", None, None),
    )
    return jax.shard_map(
        on_device, mesh=mesh, in_specs=placed, out_specs=P(None, "facet"), check_vma=False
    )
```

```python
import jax
import jax.numpy as jnp
from jax import lax
from jax.experimental import pallas as pl
from jax.experimental.pallas import tpu as pltpu
from jax.sharding import PartitionSpec as P

STRIP = 128
VISB = 128
TERMS = 2
ITERS = 2
NX = 4
NY = 8
NZ = 8
PLANE = NY * NZ
OWNERS = 2 * NX * PLANE
PIECE = 8
NEAR = 2 * NX
GROUP = 4 * NEAR
BLOCKS = PLANE * NEAR
READS = 4 * BLOCKS
HALF = 64

FLAGGED = 1024.0

shrinkage = 0.05
MESH = pl.DeviceIdType.MESH


class Place:
    def __init__(self):
        chan = lax.axis_index("chan")
        facet = lax.axis_index("facet")
        self.chan, self.facet = chan, facet
        self.y, self.x = chan // NX, chan % NX
        self.z, self.core = facet // 2, facet % 2
        self.spot = self.y * NZ + self.z
        self.owner = self.core * NX + self.x
        self.ys = [lax.rem(self.y + d, NY) for d in range(NY)]
        self.zs = [lax.rem(self.z + d, NZ) for d in range(NZ)]
        self.xs = [lax.rem(self.x + d, NX) for d in range(NX)]
        self.chan_y = [yy * NX + self.x for yy in self.ys]
        self.facet_z = [zz * 2 + self.core for zz in self.zs]
        self.partner = (chan, self.z * 2 + (1 - self.core))

    def on_x(self, dx):
        return (self.y * NX + self.xs[dx], self.facet)

    def on_plane(self, dy, dz):
        return self.ys[dy] * NZ + self.zs[dz], (self.chan_y[dy], self.facet_z[dz])

    def on_chan(self, dy, dx):
        return (self.ys[dy] * NX + self.xs[dx], self.facet)

    def near(self, i):
        core = lax.rem(self.core + lax.rem(i, 2), 2)
        step = i // 2
        xx = lax.rem(self.x + step * (step + 1) // 2, NX)
        return core * NX + xx, (self.y * NX + xx, self.z * 2 + core)


def reach(d, length):
    return min(d, length - d)


FAR_FIRST = sorted(
    ((dy, dz) for dy in range(NY) for dz in range(NZ) if dy or dz),
    key=lambda step: -reach(step[0], NY) - reach(step[1], NZ),
)
CHAN_FAR_FIRST = sorted(
    ((dy, dx) for dy in range(NY) for dx in range(NX) if dy or dx),
    key=lambda step: -reach(step[0], NY) - reach(step[1], NX),
)


ROWS_NEAR = sorted(range(NY), key=lambda d: reach(d, NY))
ROWS_FAR = ROWS_NEAR[::-1]
COLUMNS_FAR = sorted(range(NZ), key=lambda d: -reach(d, NZ))
BLOCK_STEPS = ((2, 0), (1, 0), (2, 1), (3, 0), (1, 1), (3, 1), (0, 0), (0, 1))


def pick(step, values):
    value = values[0]
    for at, other in enumerate(values[1:], 1):
        value = jnp.where(step == at, other, value)
    return value


def remote(src, dst, sems, at, target):
    return pltpu.make_async_remote_copy(
        src_ref=src,
        dst_ref=dst,
        send_sem=sems.at[0, at],
        recv_sem=sems.at[1, at],
        device_id=target,
        device_id_type=MESH,
    )


def greet(targets):
    barrier = pltpu.get_barrier_semaphore()
    for target in targets:
        pl.semaphore_signal(barrier, inc=1, device_id=target, device_id_type=MESH)
    return lambda: pl.semaphore_wait(barrier, len(targets))


def owner_order(strip):
    quarter = strip % 4
    core = strip // 4 % 2
    z = strip // 8 % 8
    low_row = strip // 64 % 2
    x = strip // 128 % 4
    y = strip // 512
    return (((core * NX + x) * NY + y) * NZ + z) * PIECE + low_row * 4 + quarter


def widen(core, sky_ref, strips):
    @pl.loop(core * (OWNERS // 16), (core + 1) * (OWNERS // 16))
    def _(i):
        block = sky_ref[pl.ds(i * 8, 8)].astype(jnp.float32)
        strips[pl.ds(pl.multiple_of(i * 64, 64), 64)] = block.reshape(64, STRIP)


def gather_rows(index_smem, strips, picked):
    @pl.loop(0, PLANE)
    def _(k):
        for i in range(NEAR):
            for q in range(4):
                strip = index_smem[k, 0, 4 * i + q]
                picked[q, k, pl.ds(i, 1)] = strips[pl.ds(strip, 1)]


def selectors(index_ref, high_rows, low_hits):
    group = lax.broadcasted_iota(jnp.int32, (1, STRIP), 1) // GROUP
    row = lax.broadcasted_iota(jnp.int32, (HALF, STRIP), 0)
    for m in range(READS // STRIP):
        number = index_ref[4 * m]
        for part in range(1, 4):
            number = jnp.where(group == part, index_ref[4 * m + part], number)
        high = number // HALF
        high_rows[m] = jnp.broadcast_to(high, (16, STRIP))
        low = jnp.broadcast_to(number - high * HALF, (HALF, STRIP))
        low_hits[:, m * STRIP : (m + 1) * STRIP] = jnp.where(low == row, 1.0, 0.0).astype(jnp.bfloat16)


def scatter_block(block, high_rows, low_hits, hits, adjoint_low):
    for h in range(PLANE * PIECE // HALF):
        for m in range(READS // STRIP):
            lanes = slice(m * STRIP, (m + 1) * STRIP)
            here = jnp.where(high_rows[m] == block * (PLANE * PIECE // HALF) + h, 1.0, 0.0).astype(jnp.bfloat16)
            here = jnp.concatenate([here] * (HALF // 16), axis=0)
            hits[h * HALF : (h + 1) * HALF, lanes] = here * low_hits[:, lanes]
    return jnp.dot(hits[...], adjoint_low[...], preferred_element_type=jnp.float32)


class Named:
    def __init__(self, names, refs):
        for name, ref in zip(names, refs):
            setattr(self, name, ref)


def scratch_shapes(vis_shape, kernel_shape):
    vmem = pltpu.VMEM
    dma = pltpu.SemaphoreType.DMA
    low, wide, whole = jnp.bfloat16, jnp.float32, jnp.int32
    blocks = (NX, PLANE, PIECE, STRIP)
    index = (PLANE, 1, STRIP)
    shapes = dict(
        estimate=vmem((PIECE, STRIP), wide),
        start=vmem((PIECE, STRIP), low),
        numbers=vmem((NZ * 4, STRIP), whole),
        near_numbers=vmem((NEAR, NZ * 4, STRIP), whole),
        packed=vmem(index, wide),
        index_in=vmem(index, wide),
        index_now=vmem(index, whole),
        index_smem=pltpu.SMEM(index, whole),
        mixed=vmem((4 * 2 * NZ, STRIP), wide),
        vis_send=vmem((OWNERS, 4, STRIP), low),
        vis_near=vmem((NEAR * PLANE, 4, STRIP), low),
        vis_in=vmem((PLANE, NEAR, 4, STRIP), low),
        observed=vmem((READS, STRIP), wide),
        strips=vmem((OWNERS * PIECE, STRIP), wide),
        picked=vmem((4, PLANE, NEAR, STRIP), wide),
        adjoint=vmem((READS, STRIP), wide),
        adjoint_low=vmem((READS, STRIP), low),
        high_rows=vmem((READS // STRIP, 16, STRIP), whole),
        low_hits=vmem((HALF, READS), low),
        hits=vmem((PLANE * PIECE, READS), low),
        image=vmem((OWNERS, PIECE, STRIP), low),
        final_image=vmem((NY * NX * PIECE, STRIP), wide),
        to_chan=dma((2, 1)),
        to_meta_near=dma((2, NEAR)),
        to_meta_plane=dma((2, 1)),
        to_vis_near=dma((2, NEAR)),
        to_vis_plane=dma((2, 1)),
        local=dma((5,)),
        vis_own=vmem(vis_shape, low),
        weights=vmem(kernel_shape, low),
        start_rows=vmem((8, 4 * STRIP), wide),
    )
    for it in range(ITERS):
        shapes.update(
            {
                f"sky{it}": vmem((OWNERS, PIECE, STRIP), low),
                f"to_sky_plane{it}": dma((2, NY)),
                f"to_sky_x{it}": dma((2, NX * NY)),
                f"to_sky_pair{it}": dma((2, NX)),
                f"got_pair{it}": vmem(blocks, low),
                f"sum_pair{it}": vmem(blocks, low),
                f"got_x{it}": vmem(blocks, low),
                f"sum_x{it}": vmem(blocks[1:], low),
                f"got_plane{it}": vmem(blocks[1:], low),
                f"to_pair{it}": dma((2, NX)),
                f"to_x{it}": dma((2, NX * NY)),
                f"to_plane{it}": dma((2, 1)),
            }
        )
    return shapes


def of_iteration(s, it):
    names = [name[:-1] for name in vars(s) if name.endswith(str(it))]
    return Named(names, [getattr(s, name + str(it)) for name in names])


def prepare(me, s, index_ref, counts_ref):
    for quarter in range(4):
        columns = slice(quarter * STRIP, (quarter + 1) * STRIP)
        s.mixed[:8] = s.start_rows[:, columns]
        for low in range(2):
            s.estimate[4 * low + quarter : 4 * low + quarter + 1] = s.mixed[pl.ds(me.chan % 4 * 2 + low, 1)]
    s.start[...] = s.estimate[...].astype(jnp.bfloat16)
    s.sky0[me.owner * PLANE + me.spot] = s.estimate[...].astype(jnp.bfloat16)
    channels = index_ref.shape[1]
    s.numbers[...] = jnp.zeros(s.numbers.shape, jnp.int32)
    s.numbers[:, :channels] = owner_order(index_ref[...])
    lane = lax.broadcasted_iota(jnp.int32, (2 * NZ, STRIP), 1)
    for y in range(NY):
        for x in range(NX):
            for ch in range(2):
                chan = (y * NX + x) * 2 + ch
                live = lane < counts_ref[:, chan : chan + 1]
                for half in range(2):
                    block = s.vis_own[chan, :, half * STRIP : (half + 1) * STRIP].astype(jnp.float32)
                    s.mixed[pl.ds(ch * 2 + half, 2 * NZ, stride=4)] = jnp.where(live, block, FLAGGED)
            for z in range(NZ):
                for core in range(2):
                    row = (z * 2 + core) * 4
                    owner = ((core * NX + x) * NY + y) * NZ + z
                    s.vis_send[owner] = s.mixed[row : row + 4].astype(jnp.bfloat16)


class SkySpread:
    def __init__(self, me, t, source=None):
        self.me, self.t = me, t
        own = t.sky.at[me.owner * PLANE + me.spot]
        for dy, dz in FAR_FIRST:
            remote(own if source is None else source, own, t.to_sky_plane, dy, me.on_plane(dy, dz)[1]).start()

    def row(self, dx, dy):
        me = self.me
        return self.t.sky.at[pl.ds(((me.core * NX + me.xs[dx]) * NY + me.ys[-dy % NY]) * NZ, NZ)]

    def plane(self, dy):
        rows = self.t.sky.at[pl.ds(self.me.owner * PLANE, NZ - 1)] if dy == 0 else self.row(0, dy)
        return remote(rows, rows, self.t.to_sky_plane, dy, self.me.partner)

    def across(self, dx, dy):
        row = self.row(0, dy)
        return remote(row, row, self.t.to_sky_x, dx * NY + dy, self.me.on_x(dx))

    def pair(self, dx, dy):
        row = self.row(dx, dy)
        return remote(row, row, self.t.to_sky_pair, dx, self.me.partner)

    def whole_pair(self, dx):
        block = self.t.sky.at[pl.ds((self.me.core * NX + self.me.xs[dx]) * PLANE, PLANE)]
        return remote(block, block, self.t.to_sky_pair, dx, self.me.partner)

    def pass_rows(self):
        for dy in ROWS_NEAR:
            self.plane(dy).wait_recv()
            for dx in (2, 1, 3):
                self.across(dx, dy).start()
            self.pair(0, dy).start()

    def pass_blocks(self):
        for dy in ROWS_NEAR:
            for dx in (1, 3, 2):
                self.across(dx, dy).wait_recv()
                self.pair(NX - dx, dy).start()

    def arrived(self):
        for dx in range(NX):
            self.whole_pair(dx).wait_recv()

    def finish(self):
        for dy in range(NY):
            self.plane(dy).wait_send()
            for dx in range(1, NX):
                self.across(dx, dy).wait_send()
        for dx in range(NX):
            self.whole_pair(dx).wait_send()


def pack_numbers(me, s):
    lane = lax.broadcasted_iota(jnp.int32, (PLANE, STRIP), 1)
    place = lax.broadcasted_iota(jnp.int32, (PLANE, STRIP), 0)
    belongs = (lane // 2) == (place // NZ) * NX + me.x
    column = lax.broadcasted_iota(jnp.int32, (STRIP, STRIP), 1)
    source = lax.broadcasted_iota(jnp.int32, (STRIP, STRIP), 0)
    total = jnp.zeros((2 * PLANE, STRIP), jnp.float32)
    for i in range(NEAR):
        held = s.numbers if i == 0 else s.near_numbers.at[i]
        for j in range(TERMS):
            strips = held[pl.ds(me.core * 2 + j, NZ, stride=4)]
            high = strips // 64
            low = strips - 64 * high
            spread = jnp.concatenate(
                [
                    jnp.where(belongs, jnp.concatenate([part.astype(jnp.float32)] * NY, axis=0), 0.0)
                    for part in (high, low)
                ],
                axis=0,
            )
            move = jnp.where(column % GROUP == 4 * i + 2 * (source % 2) + j, 1.0, 0.0).astype(jnp.bfloat16)
            total += jnp.dot(spread.astype(jnp.bfloat16), move, preferred_element_type=jnp.float32)
    rows = 64.0 * total[:PLANE] + total[PLANE:]
    for d in range(PLANE):
        s.packed[d] = rows[d : d + 1]
    s.index_in[0] = s.packed[me.spot]


def exchange(me, s):
    t = of_iteration(s, 0)
    own_vis = pltpu.make_async_copy(
        s.vis_send.at[pl.ds(me.owner * PLANE, PLANE)], s.vis_near.at[pl.ds(0, PLANE)], s.local.at[0]
    )
    own_vis.start()

    def near_meta(i):
        return remote(s.numbers, s.near_numbers.at[i], s.to_meta_near, i, me.near(i)[1])

    def near_vis(i):
        owner, target = me.near(i)
        block = s.vis_send.at[pl.ds(owner * PLANE, PLANE)]
        return remote(block, s.vis_near.at[pl.ds(i * PLANE, PLANE)], s.to_vis_near, i, target)

    for i in range(1, NEAR):
        near_meta(i).start()
    for i in range(1, NEAR):
        near_vis(i).start()
    spread = SkySpread(me, t, s.start)
    own_vis.wait()

    def forward(i):
        base = i * PLANE
        s.vis_in[0, i] = s.vis_near[base + me.spot]
        for dy, dz in FAR_FIRST:
            place, target = me.on_plane(dy, dz)
            remote(s.vis_near.at[base + place], s.vis_in.at[dy * NZ + dz, i], s.to_vis_plane, 0, target).start()

    forward(0)
    for i in range(1, NEAR):
        near_meta(i).wait_recv()
    pack_numbers(me, s)
    for dy, dz in FAR_FIRST:
        spot, target = me.on_plane(dy, dz)
        remote(s.packed.at[spot], s.index_in.at[dy * NZ + dz], s.to_meta_plane, 0, target).start()
    @pl.loop(1, 6)
    def _(i):
        near_vis(i).wait_recv()
        forward(i)

    spread.pass_rows()

    @pl.loop(6, NEAR)
    def _(i):
        near_vis(i).wait_recv()
        forward(i)

    far_index = s.index_in.at[pl.ds(1, PLANE - 1)]
    all_index = remote(far_index, far_index, s.to_meta_plane, 0, me.partner)
    all_index.wait_recv()
    s.index_now[...] = jnp.clip(s.index_in[...].astype(jnp.int32), 0, OWNERS * PIECE - 1)
    to_smem = pltpu.make_async_copy(s.index_now, s.index_smem, s.local.at[1])
    to_smem.start()
    selectors(s.index_now, s.high_rows, s.low_hits)
    spread.pass_blocks()
    to_smem.wait()
    widen(me.core, t.sky, s.strips)
    spread.arrived()
    widen(1 - me.core, t.sky, s.strips)
    gather_rows(s.index_smem, s.strips, s.picked)

    arrived = s.vis_in.at[pl.ds(1, PLANE - 1)]
    all_vis = remote(arrived, arrived, s.to_vis_plane, 0, me.partner)
    all_vis.wait_recv()

    @pl.loop(0, PLANE)
    def _(k):
        rows = pl.ds(pl.multiple_of(k * 4 * NEAR, 4 * NEAR), 4 * NEAR)
        s.observed[rows] = s.vis_in[k].astype(jnp.float32).reshape(4 * NEAR, STRIP)

    def finish():
        all_index.wait_send()
        all_vis.wait_send()
        spread.finish()
        for i in range(1, NEAR):
            near_meta(i).wait_send()
            near_vis(i).wait_send()

    return finish


def back_projected(s, kernel_ref):
    for ch in range(2):
        weights = kernel_ref[ch, 0]
        gathered = jnp.concatenate(
            [s.picked[2 * ch + j].reshape(BLOCKS, STRIP).astype(jnp.bfloat16) for j in range(TERMS)], axis=1
        )
        predicted = jnp.dot(gathered, weights, preferred_element_type=jnp.float32)
        halves = []
        for half in range(2):
            observed = s.observed[pl.ds(2 * ch + half, BLOCKS, stride=4)]
            model = predicted[:, half * STRIP : (half + 1) * STRIP]
            halves.append(jnp.where(observed < FLAGGED, model - observed, 0.0).astype(jnp.bfloat16))
        residual = jnp.concatenate(halves, axis=1)
        back = lax.dot_general(residual, weights, (((1,), (1,)), ((), ())), preferred_element_type=jnp.float32)
        for j in range(TERMS):
            s.adjoint[pl.ds(2 * ch + j, BLOCKS, stride=4)] = back[:, j * STRIP : (j + 1) * STRIP]

    @pl.loop(0, READS // 128)
    def _(i):
        rows = pl.ds(pl.multiple_of(i * 128, 128), 128)
        s.adjoint_low[rows] = s.adjoint[rows].astype(jnp.bfloat16)


def reduce_gradient(me, s, it):
    t = of_iteration(s, it)

    def pair_copy(dx):
        block = s.image.at[pl.ds(((1 - me.core) * NX + lax.rem(me.x + dx, NX)) * PLANE, PLANE)]
        return remote(block, t.got_pair.at[dx], t.to_pair, dx, me.partner)

    def x_copy(dx, dy):
        target = (me.y * NX + lax.rem(me.x + dx, NX), me.facet)
        row = pl.ds(me.ys[dy] * NZ, NZ)
        return remote(t.sum_pair.at[dx, row], t.got_x.at[dx, row], t.to_x, dx * NY + dy, target)

    @pl.loop(0, 2 * NX)
    def _(step):
        dx = pick(step, [shift for shift, _ in BLOCK_STEPS])
        own = pick(step, [mine for _, mine in BLOCK_STEPS])
        core = lax.rem(me.core + 1 + own, 2)
        block = core * NX + lax.rem(me.x + dx, NX)
        part = scatter_block(block, s.high_rows, s.low_hits, s.hits, s.adjoint_low)
        s.image[pl.ds(block * PLANE, PLANE)] = part.reshape(PLANE, PIECE, STRIP).astype(jnp.bfloat16)

        @pl.when(own == 0)
        def _():
            pair_copy(dx).start()

        @pl.when(jnp.logical_and(own == 1, dx > 0))
        def _():
            pair_copy(dx).wait_recv()
            for dy in ROWS_FAR:
                row = pl.ds(me.ys[dy] * NZ, NZ)
                mine = s.image[pl.ds(block * PLANE + me.ys[dy] * NZ, NZ)].astype(jnp.float32)
                t.sum_pair[dx, row] = (mine + t.got_pair[dx, row].astype(jnp.float32)).astype(jnp.bfloat16)
                x_copy(dx, dy).start()

    pair_copy(0).wait_recv()
    for dy in ROWS_FAR:
        row = pl.ds(me.ys[dy] * NZ, NZ)
        total = s.image[pl.ds(me.owner * PLANE + me.ys[dy] * NZ, NZ)].astype(jnp.float32)
        total += t.got_pair[0, row].astype(jnp.float32)
        for dx in (2, 1, 3):
            x_copy(dx, dy).wait_recv()
            total += t.got_x[dx, row].astype(jnp.float32)
        t.sum_x[row] = total.astype(jnp.bfloat16)
        for dz in COLUMNS_FAR:
            if dy or dz:
                place, target = me.on_plane(dy, dz)
                remote(t.sum_x.at[place], t.got_plane.at[dy * NZ + dz], t.to_plane, 0, target).start()
    others = t.got_plane.at[pl.ds(1, PLANE - 1)]
    all_plane = remote(others, others, t.to_plane, 0, me.partner)
    all_plane.wait_recv()
    parts = [t.sum_x[me.spot].astype(jnp.float32)] + [jnp.zeros((PIECE, STRIP), jnp.float32) for _ in range(3)]
    for k in range(1, PLANE):
        parts[k % 4] += t.got_plane[k].astype(jnp.float32)

    def finish():
        for dx in range(NX):
            pair_copy(dx).wait_send()
        for dx in range(1, NX):
            for dy in range(NY):
                x_copy(dx, dy).wait_send()
        all_plane.wait_send()

    return (parts[0] + parts[1]) + (parts[2] + parts[3]), finish


def reconstruct_kernel(step_size, names, start_ref, index_ref, counts_ref, vis_ref, kernel_ref, out_ref, *scratch):
    s = Named(names, scratch)
    me = Place()
    rows = pl.ds(pl.multiple_of(me.chan // 4 * 8, 8), 8)
    loads = [
        pltpu.make_async_copy(source, target, s.local.at[2 + at])
        for at, (source, target) in enumerate(
            ((start_ref.at[rows], s.start_rows), (vis_ref, s.vis_own), (kernel_ref, s.weights))
        )
    ]
    for load in loads:
        load.start()
    wait_for_all = greet(
        [me.on_plane(dy, dz)[1] for dy, dz in FAR_FIRST]
        + [me.on_chan(dy, dx) for dy, dx in CHAN_FAR_FIRST if dy and dx]
        + [me.near(i)[1] for i in range(1, NEAR)]
    )
    for load in loads[:2]:
        load.wait()
    prepare(me, s, index_ref, counts_ref)
    wait_for_all()
    waits = [exchange(me, s)]
    for it in range(ITERS):
        if it:
            gather_rows(s.index_smem, s.strips, s.picked)
        else:
            loads[2].wait()
        back_projected(s, s.weights)
        gradient, finish = reduce_gradient(me, s, it)
        estimate = jnp.maximum(s.estimate[...] - step_size * gradient - shrinkage, 0.0)
        if it == ITERS - 1:
            mine = s.final_image.at[pl.ds(pl.multiple_of(me.chan * PIECE, PIECE), PIECE)]
            mine[...] = estimate
            for dy, dx in CHAN_FAR_FIRST:
                remote(mine, mine, s.to_chan, 0, me.on_chan(dy, dx)).start()
            rest = s.final_image.at[pl.ds(0, (NY * NX - 1) * PIECE)]
            remote(rest, rest, s.to_chan, 0, me.partner).wait()
            for quarter in range(4):
                columns = slice(quarter * STRIP, (quarter + 1) * STRIP)
                out_ref[:, columns] = s.final_image[pl.ds(quarter, 2 * NY * NX, stride=4)]
            waits.append(finish)
        else:
            t = of_iteration(s, it + 1)
            t.sky[me.owner * PLANE + me.spot] = estimate.astype(jnp.bfloat16)
            spread = SkySpread(me, t)
            s.estimate[...] = estimate
            finish()
            spread.pass_rows()
            spread.pass_blocks()
            widen(me.core, t.sky, s.strips)
            spread.arrived()
            widen(1 - me.core, t.sky, s.strips)
            waits.append(spread.finish)
    for finish in waits:
        finish()


def on_device(start_image, visibilities, strip_index, live_counts, uv_kernels):
    slot_count = lax.axis_size("chan") * lax.axis_size("facet")
    channels, uvtiles = visibilities.shape[1:3]
    step_size = OWNERS * PIECE / (2.5 * slot_count * channels * uvtiles)
    strips = strip_index.transpose(0, 2, 3, 1).reshape(uvtiles * TERMS, channels)
    counts = live_counts.transpose(0, 2, 1).reshape(uvtiles, channels)
    shapes = scratch_shapes(visibilities.shape[1:], uv_kernels.shape)

    def body(*refs):
        reconstruct_kernel(step_size, list(shapes), *refs)

    return pl.pallas_call(
        body,
        out_shape=jax.ShapeDtypeStruct(start_image.shape, jnp.float32),
        in_specs=[pl.BlockSpec(memory_space=space) for space in (pl.ANY, pltpu.VMEM, pltpu.VMEM, pl.ANY, pl.ANY)],
        out_specs=pl.BlockSpec(memory_space=pltpu.VMEM),
        scratch_shapes=list(shapes.values()),
        compiler_params=pltpu.CompilerParams(collective_id=0, has_side_effects=True),
        name="reconstruct",
    )(start_image, strips, counts, visibilities[0], uv_kernels)


def solution(mesh):
    placed = (
        P(None, "facet"),
        P(("chan", "facet"), None, None, None),
        P(("chan", "facet"), None, None, None),
        P(("chan", "facet"), None, None),
        P("chan", "facet", None, None),
    )
    return jax.shard_map(
        on_device, mesh=mesh, in_specs=placed, out_specs=P(None, "facet"), check_vma=False
    )
```
